128 devices in a mesh: ang: 64 (over z, y_hi, x, core), rad: 2 (over y_lo).
Axes of the slice: x: 4, y: 4 (y_hi: 2, y_lo: 2; y = y_hi * 2 + y_lo), z: 4, core: 2. Of those that a mesh axis runs over, the one named last changes fastest.
Arguments:
- wave_function: float32 [2, 2, 256, 256, 256], P(None, None, 'ang', 'rad'), may hold values from -6 to 6
- potential: float32 [256, 256, 256], P('ang', 'rad'), may hold values from -3.140625 to 3.140625
Outputs:
- evolved: float32 [2, 2, 256, 256, 256], P(None, None, 'ang', 'rad')
The draws below stay inside these ranges and needn't reach their ends.
All inputs are finite; a program needn't handle non-finite values.
Results may differ from the reference program's by a relative error of at most 0.00009.
Values sent between devices are 32-bit elements; how exact they have to be, the bound alone decides.
No kernel may reach another device: no remote copies, remote signals or barrier semaphores. Data moves between devices by JAX's collectives and lax.ppermute only.
A program may use at most 192 MiB of HBM per device.

```python
import math
import jax
import jax.numpy as jnp
from jax import lax

SPFS = 2
NZ = 256
NA = 256
NR = 256


def level_of(own_key, shape, cuts, least, high):
    def one(dim, parts):
        heights = jax.random.uniform(jax.random.fold_in(jax.random.fold_in(own_key, 6), dim), (parts,), jnp.float32, least / len(cuts), high / len(cuts))
        return jnp.repeat(jnp.exp(heights), shape[dim] // parts).reshape((-1,) + (1,) * (len(shape) - dim - 1))

    loudness = one(*cuts[0])
    for cut in cuts[1:]:
        loudness = loudness * one(*cut)
    return loudness


def gaussian(rng, shape, width, limit, shards=(), kind=jnp.bfloat16):
    drawn = width * jax.random.normal(rng, shape, jnp.float32)
    if shards:
        drawn = drawn * level_of(rng, shape, shards, -0.22, 0.18)
    return jnp.clip(drawn, -limit, limit).astype(kind)


def setup_inputs(seed: int = 0) -> dict:
    seeds = jax.random.split(jax.random.key(seed), 3)
    wave_function = gaussian(seeds[0], (2, SPFS, NA, NR, NZ), 1.0, 6.0, ((2, 64), (3, 2)), jnp.float32)
    potential = jnp.clip(jax.random.uniform(seeds[1], (NA, NR, NZ), jnp.float32, -3.140625, 3.140625), -3.140625, 3.140625)
    return dict(wave_function=wave_function, potential=potential)


highest = lax.Precision.HIGHEST
radial_rate = 0.25
axial_rate = 1.5
band_weight = 0.1
angle_scale = 100000.0
inner_radius = 1.0
outer_radius = 10.0

def rotate_pair(field_pair, cosine, sine_values):
    real_part = cosine * field_pair[0] + sine_values * field_pair[1]
    imag_part = cosine * field_pair[1] - sine_values * field_pair[0]
    return jnp.stack([real_part, imag_part])

def laplacian_from(padded, field):
    extent = field.shape[-2]
    outer = padded[..., 0:extent, :] + padded[..., 4:extent + 4, :]
    inner = padded[..., 1:extent + 1, :] + padded[..., 3:extent + 3, :]
    return (16.0 * inner - outer - 30.0 * field) / 12.0

def radial_advance(field_pair, laplacian):
    flip_sign = jnp.array([1.0, -1.0], dtype=jnp.float32).reshape((2,) + (1,) * (field_pair.ndim - 1))
    result_sum = field_pair
    summand = field_pair
    for degree in range(1, 4):
        summand = radial_rate / degree * flip_sign * jnp.flip(laplacian(summand), 0)
        result_sum = result_sum + summand
    return result_sum

def sine_matrix(extent):
    ordinal = jnp.arange(extent, dtype=jnp.int32) + 1
    product = ordinal[:, None] * ordinal[None, :] % (2 * (extent + 1))
    return math.sqrt(2.0 / (extent + 1)) * jnp.sin(math.pi * product.astype(jnp.float32) / (extent + 1))

def axial_advance(field_pair):
    extent = field_pair.shape[-1]
    matrix_values = sine_matrix(extent)
    ordinal = (jnp.arange(extent, dtype=jnp.int32) + 1).astype(jnp.float32)
    stiffness = axial_rate * (2.0 - 2.0 * jnp.cos(math.pi * ordinal / (extent + 1)))
    denominator = 1.0 + stiffness * stiffness
    gain_real = (1.0 - stiffness * stiffness) / denominator
    gain_imag = -2.0 * stiffness / denominator
    spectrum = jnp.matmul(field_pair, matrix_values, precision=highest)
    turned = jnp.stack([gain_real * spectrum[0] - gain_imag * spectrum[1], gain_real * spectrum[1] + gain_imag * spectrum[0]])
    return jnp.matmul(turned, matrix_values, precision=highest)

def angle_coefficient(radius_index, radial_total):
    radius_value = inner_radius + (outer_radius - inner_radius) * (radius_index.astype(jnp.float32) + 0.5) / radial_total
    return angle_scale / (radius_value * radius_value)

def fourier_tables(extent):
    ordinal = jnp.arange(extent, dtype=jnp.int32)
    phase = 2.0 * math.pi * (ordinal[:, None] * ordinal[None, :] % extent).astype(jnp.float32) / extent
    return (jnp.cos(phase), jnp.sin(phase))

def spectral_solve(banded, coefficient):
    extent = banded.shape[-2]
    cosine, sine_values = fourier_tables(extent)

    def transform(matrix_values, field):
        return jnp.matmul(matrix_values, field, precision=highest)
    freq_real = transform(cosine, banded[0]) + transform(sine_values, banded[1])
    freq_imag = transform(cosine, banded[1]) - transform(sine_values, banded[0])
    base_cosine = cosine[:, 1:2]
    band_value = 1.0 + 2.0 * band_weight * base_cosine
    second = coefficient * (2.0 * base_cosine - 2.0)
    denominator = band_value * band_value + second * second
    inverse_real = band_value / denominator
    inverse_imag = second / denominator
    solved_real = freq_real * inverse_real - freq_imag * inverse_imag
    solved_imag = freq_real * inverse_imag + freq_imag * inverse_real
    back_real = (transform(cosine, solved_real) - transform(sine_values, solved_imag)) / extent
    back_imag = (transform(cosine, solved_imag) + transform(sine_values, solved_real)) / extent
    return jnp.stack([back_real, back_imag])

def reference(wave_function, potential):
    cosine = jnp.cos(potential)
    sine_values = jnp.sin(potential)
    radius_index = jnp.arange(NR, dtype=jnp.int32)
    column_coefficient = jnp.repeat(angle_coefficient(radius_index, NR), NZ)

    def laplacian(summand):
        padding = [(0, 0)] * (summand.ndim - 2) + [(2, 2), (0, 0)]
        return laplacian_from(jnp.pad(summand, padding), summand)

    def evolve_single(field_pair):
        rotated = rotate_pair(field_pair, cosine, sine_values)
        radial = radial_advance(rotated, laplacian)
        axial = axial_advance(radial)
        banded = band_weight * (jnp.roll(axial, 1, axis=1) + jnp.roll(axial, -1, axis=1)) + axial
        solved = spectral_solve(banded.reshape(2, NA, NR * NZ), column_coefficient).reshape(axial.shape)
        return rotate_pair(2.0 * solved - axial, cosine, sine_values)
    stacked = jnp.moveaxis(wave_function, 1, 0)
    return jnp.moveaxis(lax.map(evolve_single, stacked), 0, 1)
```

```python
import functools

import jax
import jax.numpy as jnp
import numpy as np
from jax import lax
from jax.experimental import pallas as pl
from jax.experimental.pallas import tpu as pltpu
from jax.sharding import PartitionSpec as P

NA = 256
NR = 256
NZ = 256
CHIPS = 32
LR = 128
f32 = jnp.float32
bf16 = jnp.bfloat16


def split(a):
    hi = np.asarray(a, np.float32).astype(jnp.bfloat16)
    lo = (np.asarray(a, np.float64) - hi.astype(np.float64)).astype(np.float32)
    return hi, lo.astype(jnp.bfloat16)


def coefficients():
    j = np.arange(NR, dtype=np.float32)
    radius = np.float32(1.0) + np.float32(9.0) * (j + np.float32(0.5)) / np.float32(NR)
    return (np.float32(100000.0) / (radius * radius)).astype(np.float64)


def radial_tables():
    lap = np.zeros((NR, NR))
    for d, c in ((0, -30.0), (1, 16.0), (2, -1.0)):
        for j in range(NR - d):
            lap[j, j + d] = c / 12.0
            lap[j + d, j] = c / 12.0
    k = 0.25 * lap
    even = np.eye(NR) - k @ k / 2.0
    odd = -k + k @ k @ k / 6.0
    main, halo = [], []
    for side in range(2):
        own = slice(LR * side, LR * side + LR)
        a, b = even[own, own], odd[own, own]
        hi, lo = split(np.block([[a, -b], [b, a]]))
        main.append(np.concatenate([hi, hi, lo], axis=1))
        rows = slice(120, 128) if side == 0 else slice(128, 136)
        cols = slice(128, 136) if side == 0 else slice(120, 128)
        a, b = even[rows, cols], odd[rows, cols]
        halo.append(np.block([[a, -b], [b, a]]))
    return np.stack(main), np.stack(halo).astype(np.float32)


def axial_tables():
    n = np.arange(1, NZ + 1)
    sine = np.sqrt(2.0 / (NZ + 1)) * np.sin(np.pi * (n[:, None] * n[None, :]) / (NZ + 1))
    s = 1.5 * (2.0 - 2.0 * np.cos(np.pi * n / (NZ + 1)))
    gain = (1.0 - 1j * s) / (1.0 + 1j * s)
    full = (sine * gain[None, :]) @ sine
    re, im = full.real, full.imag
    return split(np.block([[re, im], [-im, re]]))


def dirichlet(c, size):
    off = 0.1 - 1j * c
    mat = np.zeros((size, size), complex)
    for t in range(size):
        mat[t, t] = 1.0 + 2j * c
        if t:
            mat[t, t - 1] = off
            mat[t - 1, t] = off
    inv = np.linalg.inv(mat)
    return inv, -off * inv[:, 0]


def angle_tables():
    cell = np.zeros((2, LR, 128), np.float32)
    chip = np.zeros((2, 2, 64, 8, 128), np.float32)
    mid = np.zeros((2, 2, 32, 8, 128), np.float32)
    angle = np.arange(NA)
    second = 2.0 * np.cos(2.0 * np.pi * angle / NA) - 2.0
    for g, c in enumerate(coefficients()):
        rho = 0.1 / (0.1 - 1j * c)
        scale = 2.4 * (1.0 - rho)
        inv, p = dirichlet(c, 3)
        w0 = 2.0 * rho - 1.0
        values = [
            (p[0] + p[2]) / 2,
            (p[0] - p[2]) / 2,
            p[1],
            w0,
            (w0 + scale * (inv[0, 0] + inv[0, 2])) / 2,
            (w0 + scale * (inv[0, 0] - inv[0, 2])) / 2,
            scale * inv[0, 1],
            w0 + scale * inv[1, 1],
        ]
        side, j = divmod(g, LR)
        for k, value in enumerate(values):
            cell[side, j, 2 * k] = value.real
            cell[side, j, 2 * k + 1] = value.imag
        inv8, p8 = dirichlet(c, 7)
        core, jj = divmod(j, 64)
        sign = np.array([-1, -1, 1, 1, -1, -1, 1, 1.0])
        middle, local = p8[3], scale * inv8[3, 3]
        chip[side, core, jj, :, 0] = middle.real
        chip[side, core, jj, :, 1] = middle.imag * sign
        chip[side, core, jj, :, 2] = local.real
        chip[side, core, jj, :, 3] = local.imag * sign
        symbol = 1.0 / (1.2 + (0.1 - 1j * c) * second)
        coarse = scale * symbol.reshape(8, CHIPS).sum(0) / 8.0
        pos, r = divmod(jj, 2)
        mid[side, core, pos, 2 * r, :64] = np.repeat(coarse.real, 2)
        mid[side, core, pos, 2 * r + 1, :64] = np.repeat(coarse.imag, 2)
    return cell, chip.reshape(4, 512, 128), mid.reshape(128, 8, 128)


def fourier_tables():
    k = np.arange(CHIPS)
    q = np.arange(CHIPS)
    fwd = np.zeros((2, CHIPS, 2, CHIPS, 2, 2, 2))
    inv = np.zeros((CHIPS, 2, 2, 2, 2, CHIPS, 2))
    for n in range(2):
        phase = -2.0 * np.pi * ((k[:, None] * (q[None, :] + n)) % CHIPS) / CHIPS
        e = np.exp(1j * phase)
        for s in range(2):
            fwd[0, :, s, :, n, 0, s] = e.real
            fwd[0, :, s, :, n, 1, s] = -e.imag
            fwd[1, :, s, :, n, 0, s] = e.imag
            fwd[1, :, s, :, n, 1, s] = e.real
            d = np.conj(e).T / CHIPS
            inv[:, n, 0, s, 0, :, s] = d.real
            inv[:, n, 0, s, 1, :, s] = -d.imag
            inv[:, n, 1, s, 0, :, s] = d.imag
            inv[:, n, 1, s, 1, :, s] = d.real
    fwd = fwd.reshape(128, 256)
    inv = inv.reshape(256, 128)
    fh, fl = split(fwd)
    ih, il = split(inv)
    return np.concatenate([fh, fh, fl], axis=1), np.concatenate([ih, ih, il], axis=1)


@functools.cache
def tables():
    main, halo = radial_tables()
    ah, al = axial_tables()
    cell, chip, mid = angle_tables()
    fwd, inv = fourier_tables()
    return dict(main=main, halo=halo, ah=ah, al=al, cell=cell, chip=chip, mid=mid, fwd=fwd, inv=inv)


def dot(a, b):
    return jnp.dot(a, b, preferred_element_type=f32)


def halves(x):
    hi = x.astype(bf16)
    return hi, (x - hi.astype(f32)).astype(bf16)


def stacked(x):
    hi, lo = halves(x)
    return jnp.concatenate([hi, lo, hi], axis=0)


def times(x, high, low):
    hi, lo = halves(x)
    return dot(hi, high) + dot(lo, high) + dot(hi, low)


SIN = (
    -1.0 / 6.0,
    1.0 / 120.0,
    -1.0 / 5040.0,
    1.0 / 362880.0,
    -1.0 / 39916800.0,
    1.0 / 6227020800.0,
)
COS = (
    -1.0 / 2.0,
    1.0 / 24.0,
    -1.0 / 720.0,
    1.0 / 40320.0,
    -1.0 / 3628800.0,
    1.0 / 479001600.0,
    -1.0 / 87178291200.0,
)


def cos_sin(x):
    y = 0.5 * x
    q = y * y
    a = jnp.full_like(q, SIN[-1])
    for c in SIN[-2::-1]:
        a = a * q + c
    b = jnp.full_like(q, COS[-1])
    for c in COS[-2::-1]:
        b = b * q + c
    s = y + y * (q * a)
    c = 1.0 + q * b
    s2 = s + s
    return 1.0 - s2 * s, s2 * c


def cmul(cr, ci, x):
    return (cr * x[0] - ci * x[1], cr * x[1] + ci * x[0])


def add(x, y):
    return (x[0] + y[0], x[1] + y[1])


def sub(x, y):
    return (x[0] - y[0], x[1] - y[1])


def weights(coef, k, width):
    shape = (coef.shape[0], width)
    return tuple(jnp.broadcast_to(coef[:, i : i + 1], shape) for i in (2 * k, 2 * k + 1))


def reduce_cells(f, coef):
    width = f[0][0].shape[-1]
    s, d = add(f[1], f[3]), sub(f[1], f[3])
    even = add(cmul(*weights(coef, 0, width), s), cmul(*weights(coef, 2, width), f[2]))
    odd = cmul(*weights(coef, 1, width), d)
    return add(add(f[0], even), odd), sub(even, odd)


def advance_kernel(idx, w, pot, main, coef, f, cs, uv):
    a = pl.program_id(0)
    c, s = cos_sin(pot[0])
    cs[0, 0] = c
    cs[1, 0] = s
    for m in range(2):
        re, im = w[0, m, 0], w[1, m, 0]
        x = jnp.concatenate([c * re + s * im, c * im - s * re], axis=0)
        f[m, pl.ds(a, 1)] = dot(main[0], stacked(x)).reshape(1, 2, LR, NZ)

    @pl.when(a == 3)
    def _():
        def block(b, carry):
            rows = pl.ds(pl.multiple_of(b * 8, 8), 8)
            base = (lax.shift_right_logical(b, 3) ^ idx[1]) * 1024 + (b & 7) * 128
            k = coef[0, rows, :]
            for m in range(2):
                u, v = reduce_cells([(f[m, t, 0, rows, :], f[m, t, 1, rows, :]) for t in range(4)], k)
                for i, value in enumerate((u[0], u[1], v[0], v[1])):
                    for z in range(2):
                        uv[pl.ds(base + 8 * z + 2 * i + m, 8, stride=16), :] = value[:, 128 * z : 128 * z + 128]
            return carry

        lax.fori_loop(0, 16, block, 0)


def halo_kernel(idx, halo, table, coef, f_in, uv_in, f, uv):
    corrections = []
    parts = []
    for t in range(4):
        c, s = cos_sin(halo[4, t])
        for m in range(2):
            re, im = halo[m, t], halo[2 + m, t]
            parts.append(jnp.concatenate([c * re + s * im, c * im - s * re], axis=0))
    x = jnp.concatenate(parts, axis=1)
    out = jnp.dot(table[0], x, precision=lax.Precision.HIGHEST, preferred_element_type=f32)
    k = coef[0]
    for m in range(2):
        cells = []
        for t in range(4):
            piece = out[:, (2 * t + m) * NZ : (2 * t + m + 1) * NZ]
            cells.append((piece[:8], piece[8:]))
            f[m, t, 0] = f_in[m, t, 0] + piece[:8]
            f[m, t, 1] = f_in[m, t, 1] + piece[8:]
        u, v = reduce_cells(cells, k)
        for i, value in enumerate((u[0], u[1], v[0], v[1])):
            for z in range(2):
                rows = pl.ds(8 * z + 2 * i + m, 8, stride=16)
                uv[rows, :] = uv_in[rows, :] + value[:, 128 * z : 128 * z + 128]


def row_swap(x, shift):
    return pltpu.roll(x, shift, 2)


def first_rows(core, shape):
    row = lax.broadcasted_iota(jnp.int32, shape, 2)
    return (lax.shift_right_logical(row, 2) ^ core) == 0


def tiles(x):
    return x.reshape(x.shape[0] // 16, 2, 8, 128)


def wide(x):
    x = tiles(x)
    rows = 8 * x.shape[0]
    return jnp.concatenate([x[:, z].reshape(rows, 128) for z in range(2)], axis=1)


def narrow(x):
    rows = x.shape[0] // 8
    return jnp.stack([x[:, 128 * z : 128 * z + 128].reshape(rows, 8, 128) for z in range(2)], axis=1)


def row_weights(chip):
    return chip[0].reshape(64, 1, 8, 128)


def pair_kernel(idx, own, received, chip, uv, m_out):
    a, b = tiles(own[...]), tiles(received[...])
    mask = first_rows(idx[1], a.shape)
    ends = jnp.where(mask, a, b)
    inner = jnp.where(mask, b, a)
    inner = inner + row_swap(inner, 4)
    k = row_weights(chip)
    out = ends + k[..., 0:1] * inner + k[..., 1:2] * row_swap(inner, 2)
    uv[...] = out.reshape(uv.shape)
    m_out[...] = inner.reshape(uv.shape)


def pair_axial_kernel(idx, m, chip, ah, al, out):
    e = times(wide(m[...]), ah[...], al[...])
    row = lax.broadcasted_iota(jnp.int32, (1, 1, 8, 128), 2)
    sign = jnp.where((row & 2) == 0, -1.0, 1.0)
    x = narrow(e[:, :NZ]) + sign * row_swap(narrow(e[:, NZ:]), 2)
    k = row_weights(chip)
    x = k[..., 2:3] * x + k[..., 3:4] * row_swap(x, 2)
    out[...] = x.reshape(out.shape)


def local_kernel(idx, f, coef, ah, al, out):
    k = coef[0]
    cells = [(f[0, t, 0], f[0, t, 1]) for t in range(4)]
    s, d = add(cells[1], cells[3]), sub(cells[1], cells[3])
    even = add(cmul(*weights(k, 4, NZ), s), cmul(*weights(k, 6, NZ), cells[2]))
    odd = cmul(*weights(k, 5, NZ), d)
    parts = [
        cmul(*weights(k, 3, NZ), cells[0]),
        add(even, odd),
        add(cmul(*weights(k, 6, NZ), s), cmul(*weights(k, 7, NZ), cells[2])),
        sub(even, odd),
    ]
    x = jnp.concatenate([jnp.concatenate(p, axis=1) for p in parts], axis=0)
    y = times(x, ah[...], al[...])
    rows = cells[0][0].shape[0]
    for t in range(4):
        out[0, t, 0] = y[t * rows : (t + 1) * rows, :NZ]
        out[0, t, 1] = y[t * rows : (t + 1) * rows, NZ:]


def middle_kernel(idx, x, fwd, inv, mid, ah, al, out):
    x = x[...].reshape(CHIPS, 2, 2, 8, 128)
    x = jnp.concatenate([x[:, r, z].reshape(256, 128) for r in range(2) for z in range(2)], axis=1)
    g = dot(fwd[...], stacked(x))
    k = mid[0].T
    rows = []
    for r in range(2):
        col = slice(r * NZ, (r + 1) * NZ)
        kr, ki = weights(k[:64], r, NZ)
        rows.append(jnp.concatenate(cmul(kr, ki, (g[:64, col], g[64:, col])), axis=1))
    h = times(jnp.concatenate(rows, axis=0), ah[...], al[...])
    h = jnp.concatenate(
        [jnp.concatenate([h[64 * r : 64 * r + 64, :NZ], h[64 * r : 64 * r + 64, NZ:]], axis=0) for r in range(2)],
        axis=1,
    )
    y = dot(inv[...], stacked(h))
    y = jnp.stack([y[:, 128 * i : 128 * i + 128].reshape(CHIPS, 8, 128) for i in range(4)], axis=1)
    out[...] = y.reshape(out.shape)


def spread_kernel(idx, y, mA, chip, keep, send):
    x = tiles(y[...])
    total = x + row_swap(x, 4)
    k = row_weights(chip)
    inner = k[..., 0:1] * total + k[..., 1:2] * row_swap(total, 2) + tiles(mA[...])
    mask = first_rows(idx[1], x.shape)
    keep[...] = jnp.where(mask, x, inner).reshape(keep.shape)
    send[...] = jnp.where(mask, inner, x).reshape(keep.shape)


def finish_kernel(idx, w, keep, received, cs, coef, out, y):
    half = lax.shift_right_logical(pl.program_id(0), 1)

    @pl.when(half == idx[1])
    def _():
        y[...] = keep[...]

    @pl.when(half != idx[1])
    def _():
        y[...] = received[...]

    k = coef[0]
    rows = k.shape[0]
    for m in range(2):
        a = [
            jnp.concatenate([y[pl.ds(8 * z + 2 * i + m, rows, stride=16), :] for z in range(2)], axis=1)
            for i in range(4)
        ]
        left, right = (a[0], a[1]), (a[2], a[3])
        s, d = add(left, right), sub(left, right)
        even = cmul(*weights(k, 0, NZ), s)
        odd = cmul(*weights(k, 1, NZ), d)
        parts = [left, add(even, odd), cmul(*weights(k, 2, NZ), s), sub(even, odd)]
        for t in range(4):
            re, im = w[m, t, 0] + parts[t][0], w[m, t, 1] + parts[t][1]
            c, sn = cs[0, t], cs[1, t]
            out[0, m, t] = c * re + sn * im
            out[1, m, t] = c * im - sn * re


def call(kernel, idx, args, in_specs, out_shape, out_specs, grid=(1,), scratch=(), aliases=None, flops=0, nbytes=0):
    return pl.pallas_call(
        kernel,
        out_shape=out_shape,
        grid_spec=pltpu.PrefetchScalarGridSpec(
            num_scalar_prefetch=1, grid=grid, in_specs=in_specs, out_specs=out_specs, scratch_shapes=scratch
        ),
        input_output_aliases=aliases or {},
        compiler_params=pltpu.CompilerParams(dimension_semantics=("arbitrary",) * len(grid)),
        cost_estimate=pl.CostEstimate(flops=flops, bytes_accessed=nbytes, transcendentals=0),
        name=kernel.__name__,
    )(idx, *args)


def whole(shape):
    return pl.BlockSpec(shape, lambda *_: (0,) * len(shape))


def body(wave, potential):
    t = tables()
    rad = lax.axis_index("rad")
    ang = lax.axis_index("ang")
    core = ang % 2
    chip = ang // 2
    lane = jnp.arange(8, dtype=jnp.int32)
    edge = jnp.where(rad == 0, 15, 0)
    edge_uv = ((edge // 8) ^ core) * 8 + edge % 8
    idx = jnp.zeros(8, jnp.int32)
    for i, v in enumerate((rad, core, chip, rad * 2 + core, rad * 64 + core * 32 + chip, edge, edge_uv)):
        idx = jnp.where(lane == i, v.astype(jnp.int32), idx)

    start = jnp.where(rad == 0, 120, 0)
    rim = lax.dynamic_slice_in_dim(wave, start, 8, axis=3).reshape(4, 4, 8, NZ)
    rim_p = lax.dynamic_slice_in_dim(potential, start, 8, axis=1).reshape(1, 4, 8, NZ)
    halo = lax.ppermute(jnp.concatenate([rim, rim_p]), "rad", [(0, 1), (1, 0)])

    sds = jax.ShapeDtypeStruct
    field = sds((2, 4, 2, LR, NZ), f32)
    lines = sds((1024, 128), f32)
    f, cs, uv = call(
        advance_kernel,
        idx,
        (wave, potential, t["main"], t["cell"]),
        [
            pl.BlockSpec((2, 2, 1, LR, NZ), lambda a, i: (0, 0, a, 0, 0)),
            pl.BlockSpec((1, LR, NZ), lambda a, i: (a, 0, 0)),
            pl.BlockSpec((1, 256, 768), lambda a, i: (i[0], 0, 0)),
            pl.BlockSpec((1, LR, 128), lambda a, i: (i[0], 0, 0)),
        ],
        (field, sds((2, 4, LR, NZ), f32), sds((2048, 128), f32)),
        (
            whole(field.shape),
            pl.BlockSpec((2, 1, LR, NZ), lambda a, i: (0, a, 0, 0)),
            whole((2048, 128)),
        ),
        grid=(4,),
        flops=1 << 30,
        nbytes=5 << 20,
    )
    f, uv = call(
        halo_kernel,
        idx,
        (halo, t["halo"], t["cell"], f, uv),
        [
            whole((5, 4, 8, NZ)),
            pl.BlockSpec((1, 16, 16), lambda a, i: (i[0], 0, 0)),
            pl.BlockSpec((1, 8, 128), lambda a, i: (i[0], i[5], 0)),
            pl.BlockSpec((2, 4, 2, 8, NZ), lambda a, i: (0, 0, 0, i[5], 0)),
            pl.BlockSpec((128, 128), lambda a, i: (i[6], 0)),
        ],
        (field, sds((2048, 128), f32)),
        (
            pl.BlockSpec((2, 4, 2, 8, NZ), lambda a, i: (0, 0, 0, i[5], 0)),
            pl.BlockSpec((128, 128), lambda a, i: (i[6], 0)),
        ),
        aliases={4: 0, 5: 1},
        flops=1 << 20,
        nbytes=1 << 20,
    )
    other = [(i, i ^ 1) for i in range(2 * CHIPS)]
    groups = [[2 * q + c for q in range(CHIPS)] for c in range(2)]
    exchange = functools.partial(
        lax.all_to_all, axis_name="ang", split_axis=0, concat_axis=0, tiled=True, axis_index_groups=groups
    )
    received = lax.ppermute(uv[1024:], "ang", other)
    chip_spec = pl.BlockSpec((1, 512, 128), lambda a, i: (i[3], 0, 0))
    lines_spec = whole((1024, 128))
    UV, m = call(
        pair_kernel,
        idx,
        (uv[:1024], received, t["chip"]),
        [lines_spec, lines_spec, chip_spec],
        (lines, lines),
        (lines_spec, lines_spec),
        flops=1 << 20,
        nbytes=2 << 20,
    )
    x = exchange(UV)
    local = call(
        local_kernel,
        idx,
        (f, t["cell"], t["ah"], t["al"]),
        [
            pl.BlockSpec((1, 4, 2, 64, NZ), lambda s, j, i: (s, 0, 0, j, 0)),
            pl.BlockSpec((1, 64, 128), lambda s, j, i: (i[0], j, 0)),
            whole((512, 512)),
            whole((512, 512)),
        ],
        field,
        pl.BlockSpec((1, 4, 2, 64, NZ), lambda s, j, i: (s, 0, 0, j, 0)),
        grid=(2, 2),
        flops=3 << 30,
        nbytes=5 << 20,
    )
    mA = call(
        pair_axial_kernel,
        idx,
        (m, t["chip"], t["ah"], t["al"]),
        [lines_spec, chip_spec, whole((256, 512)), whole((256, 512))],
        lines,
        lines_spec,
        flops=1 << 29,
        nbytes=2 << 20,
    )
    y = call(
        middle_kernel,
        idx,
        (x, t["fwd"], t["inv"], t["mid"], t["ah"], t["al"]),
        [
            lines_spec,
            whole((128, 768)),
            whole((256, 384)),
            pl.BlockSpec((1, 8, 128), lambda a, i: (i[4], 0, 0)),
            whole((512, 512)),
            whole((512, 512)),
        ],
        lines,
        lines_spec,
        flops=1 << 29,
        nbytes=3 << 20,
    )
    y = exchange(y)
    keep, send = call(
        spread_kernel,
        idx,
        (y, mA, t["chip"]),
        [lines_spec, lines_spec, chip_spec],
        (lines, lines),
        (lines_spec, lines_spec),
        flops=1 << 20,
        nbytes=2 << 20,
    )
    received = lax.ppermute(send, "ang", other)
    return call(
        finish_kernel,
        idx,
        (local, keep, received, cs, t["cell"]),
        [
            pl.BlockSpec((2, 4, 2, 32, NZ), lambda a, i: (0, 0, 0, a, 0)),
            pl.BlockSpec((512, 128), lambda a, i: (a % 2, 0)),
            pl.BlockSpec((512, 128), lambda a, i: (a % 2, 0)),
            pl.BlockSpec((2, 4, 32, NZ), lambda a, i: (0, 0, a, 0)),
            pl.BlockSpec((1, 32, 128), lambda a, i: (i[0], a, 0)),
        ],
        sds(wave.shape, f32),
        pl.BlockSpec((2, 2, 4, 32, NZ), lambda a, i: (0, 0, 0, a, 0)),
        grid=(4,),
        scratch=(pltpu.VMEM((512, 128), f32),),
        flops=1 << 22,
        nbytes=6 << 20,
    )


def solution(mesh):
    placed = (P(None, None, "ang", "rad", None), P("ang", "rad", None))
    return jax.shard_map(
        body,
        mesh=mesh,
        in_specs=placed,
        out_specs=P(None, None, "ang", "rad", None),
        check_vma=False,
    )
```

```python
import functools

import jax
import jax.numpy as jnp
import numpy as np
from jax import lax
from jax.experimental import pallas as pl
from jax.experimental.pallas import tpu as pltpu
from jax.sharding import PartitionSpec as P

NA = 256
NR = 256
NZ = 256
CHIPS = 32
LR = 128
f32 = jnp.float32
bf16 = jnp.bfloat16


def split(a):
    hi = np.asarray(a, np.float32).astype(jnp.bfloat16)
    lo = (np.asarray(a, np.float64) - hi.astype(np.float64)).astype(np.float32)
    return hi, lo.astype(jnp.bfloat16)


def coefficients():
    j = np.arange(NR, dtype=np.float32)
    radius = np.float32(1.0) + np.float32(9.0) * (j + np.float32(0.5)) / np.float32(NR)
    return (np.float32(100000.0) / (radius * radius)).astype(np.float64)


def radial_tables():
    lap = np.zeros((NR, NR))
    for d, c in ((0, -30.0), (1, 16.0), (2, -1.0)):
        for j in range(NR - d):
            lap[j, j + d] = c / 12.0
            lap[j + d, j] = c / 12.0
    k = 0.25 * lap
    even = np.eye(NR) - k @ k / 2.0
    odd = -k + k @ k @ k / 6.0
    main, halo = [], []
    for side in range(2):
        own = slice(LR * side, LR * side + LR)
        a, b = even[own, own], odd[own, own]
        hi, lo = split(np.block([[a, -b], [b, a]]))
        main.append(np.concatenate([hi, hi, lo], axis=1))
        rows = slice(120, 128) if side == 0 else slice(128, 136)
        cols = slice(128, 136) if side == 0 else slice(120, 128)
        a, b = even[rows, cols], odd[rows, cols]
        halo.append(np.block([[a, -b], [b, a]]))
    return np.stack(main), np.stack(halo).astype(np.float32)


def axial_tables():
    n = np.arange(1, NZ + 1)
    sine = np.sqrt(2.0 / (NZ + 1)) * np.sin(np.pi * (n[:, None] * n[None, :]) / (NZ + 1))
    s = 1.5 * (2.0 - 2.0 * np.cos(np.pi * n / (NZ + 1)))
    gain = (1.0 - 1j * s) / (1.0 + 1j * s)
    full = (sine * gain[None, :]) @ sine
    re, im = full.real, full.imag
    return split(np.stack([re, im - re, re + im]))


def dirichlet(c, size):
    off = 0.1 - 1j * c
    mat = np.zeros((size, size), complex)
    for t in range(size):
        mat[t, t] = 1.0 + 2j * c
        if t:
            mat[t, t - 1] = off
            mat[t - 1, t] = off
    inv = np.linalg.inv(mat)
    return inv, -off * inv[:, 0]


def angle_tables():
    cell = np.zeros((2, LR, 128), np.float32)
    chip = np.zeros((2, 2, 64, 8, 128), np.float32)
    mid = np.zeros((2, 2, 32, 8, 128), np.float32)
    angle = np.arange(NA)
    second = 2.0 * np.cos(2.0 * np.pi * angle / NA) - 2.0
    for g, c in enumerate(coefficients()):
        rho = 0.1 / (0.1 - 1j * c)
        scale = 2.4 * (1.0 - rho)
        inv, p = dirichlet(c, 3)
        w0 = 2.0 * rho - 1.0
        values = [
            (p[0] + p[2]) / 2,
            (p[0] - p[2]) / 2,
            p[1],
            w0,
            (w0 + scale * (inv[0, 0] + inv[0, 2])) / 2,
            (w0 + scale * (inv[0, 0] - inv[0, 2])) / 2,
            scale * inv[0, 1],
            w0 + scale * inv[1, 1],
        ]
        side, j = divmod(g, LR)
        for k, value in enumerate(values):
            cell[side, j, 2 * k] = value.real
            cell[side, j, 2 * k + 1] = value.imag
        inv8, p8 = dirichlet(c, 7)
        core, jj = divmod(j, 64)
        sign = np.array([-1, -1, 1, 1, -1, -1, 1, 1.0])
        middle, local = p8[3], scale * inv8[3, 3]
        chip[side, core, jj, :, 0] = middle.real
        chip[side, core, jj, :, 1] = middle.imag * sign
        chip[side, core, jj, :, 2] = local.real
        chip[side, core, jj, :, 3] = local.imag * sign
        symbol = 1.0 / (1.2 + (0.1 - 1j * c) * second)
        coarse = scale * symbol.reshape(8, CHIPS).sum(0) / 8.0
        pos, r = divmod(jj, 2)
        mid[side, core, pos, 2 * r, :64] = np.repeat(coarse.real, 2)
        mid[side, core, pos, 2 * r + 1, :64] = np.repeat(coarse.imag, 2)
    return cell, chip.reshape(4, 512, 128), mid.reshape(128, 8, 128)


def fourier_tables():
    k = np.arange(CHIPS)
    q = np.arange(CHIPS)
    fwd = np.zeros((2, CHIPS, 2, CHIPS, 2, 2, 2))
    inv = np.zeros((CHIPS, 2, 2, 2, 2, CHIPS, 2))
    for n in range(2):
        phase = -2.0 * np.pi * ((k[:, None] * (q[None, :] + n)) % CHIPS) / CHIPS
        e = np.exp(1j * phase)
        for s in range(2):
            fwd[0, :, s, :, n, 0, s] = e.real
            fwd[0, :, s, :, n, 1, s] = -e.imag
            fwd[1, :, s, :, n, 0, s] = e.imag
            fwd[1, :, s, :, n, 1, s] = e.real
            d = np.conj(e).T / CHIPS
            inv[:, n, 0, s, 0, :, s] = d.real
            inv[:, n, 0, s, 1, :, s] = -d.imag
            inv[:, n, 1, s, 0, :, s] = d.imag
            inv[:, n, 1, s, 1, :, s] = d.real
    fwd = fwd.reshape(128, 256)
    inv = inv.reshape(256, 128)
    fh, fl = split(fwd)
    ih, il = split(inv)
    return np.concatenate([fh, fh, fl], axis=1), np.concatenate([ih, ih, il], axis=1)


@functools.cache
def tables():
    main, halo = radial_tables()
    ah, al = axial_tables()
    cell, chip, mid = angle_tables()
    fwd, inv = fourier_tables()
    return dict(main=main, halo=halo, ah=ah, al=al, cell=cell, chip=chip, mid=mid, fwd=fwd, inv=inv)


def dot(a, b):
    return jnp.dot(a, b, preferred_element_type=f32)


def halves(x):
    hi = x.astype(bf16)
    return hi, (x - hi.astype(f32)).astype(bf16)


def stacked(x):
    hi, lo = halves(x)
    return jnp.concatenate([hi, lo, hi], axis=0)


def times(x, high, low):
    hi, lo = halves(x)
    return dot(hi, high) + dot(lo, high) + dot(hi, low)


def complex_times(re, im, high, low):
    p, q, r = [times(x, high[i], low[i]) for i, x in enumerate((re + im, re, im))]
    return p - r, p + q


SIN = (
    -1.0 / 6.0,
    1.0 / 120.0,
    -1.0 / 5040.0,
    1.0 / 362880.0,
    -1.0 / 39916800.0,
    1.0 / 6227020800.0,
)
COS = (
    -1.0 / 2.0,
    1.0 / 24.0,
    -1.0 / 720.0,
    1.0 / 40320.0,
    -1.0 / 3628800.0,
    1.0 / 479001600.0,
    -1.0 / 87178291200.0,
)


def cos_sin(x):
    y = 0.5 * x
    q = y * y
    a = jnp.full_like(q, SIN[-1])
    for c in SIN[-2::-1]:
        a = a * q + c
    b = jnp.full_like(q, COS[-1])
    for c in COS[-2::-1]:
        b = b * q + c
    s = y + y * (q * a)
    c = 1.0 + q * b
    s2 = s + s
    return 1.0 - s2 * s, s2 * c


def cmul(cr, ci, x):
    return (cr * x[0] - ci * x[1], cr * x[1] + ci * x[0])


def add(x, y):
    return (x[0] + y[0], x[1] + y[1])


def sub(x, y):
    return (x[0] - y[0], x[1] - y[1])


def weights(coef, k, width):
    shape = (coef.shape[0], width)
    return tuple(jnp.broadcast_to(coef[:, i : i + 1], shape) for i in (2 * k, 2 * k + 1))


def reduce_cells(f, coef):
    width = f[0][0].shape[-1]
    s, d = add(f[1], f[3]), sub(f[1], f[3])
    even = add(cmul(*weights(coef, 0, width), s), cmul(*weights(coef, 2, width), f[2]))
    odd = cmul(*weights(coef, 1, width), d)
    return add(add(f[0], even), odd), sub(even, odd)


def advance_kernel(idx, w, pot, main, coef, *refs):
    n = (len(refs) - 6) // 2
    sources, (f_out, cs, uv), targets = refs[:n], refs[n : n + 3], refs[n + 3 : -3]
    f, sems, f_sems = refs[-3:]
    a = pl.program_id(0)
    own = {1: idx[3], 2: idx[0]}
    copies = [
        pltpu.make_async_copy(x.at[own[i]] if i in own else x, y, sems.at[i])
        for i, (x, y) in enumerate(zip(sources, targets))
    ]

    @pl.when(a == 0)
    def _():
        for copy in copies:
            copy.start()

    c, s = cos_sin(pot[0])
    cs[0, 0] = c
    cs[1, 0] = s
    for m in range(2):
        re, im = w[0, m, 0], w[1, m, 0]
        x = jnp.concatenate([c * re + s * im, c * im - s * re], axis=0)
        f[m, pl.ds(a, 1)] = dot(main[0], stacked(x)).reshape(1, 2, LR, NZ)
    pltpu.make_async_copy(f.at[:, a], f_out.at[:, a], f_sems.at[a]).start()

    @pl.when(a == 3)
    def _():
        def block(b, carry):
            rows = pl.ds(pl.multiple_of(b * 8, 8), 8)
            base = (lax.shift_right_logical(b, 3) ^ idx[1]) * 1024 + (b & 7) * 128
            k = coef[0, rows, :]
            for m in range(2):
                u, v = reduce_cells([(f[m, t, 0, rows, :], f[m, t, 1, rows, :]) for t in range(4)], k)
                for i, value in enumerate((u[0], u[1], v[0], v[1])):
                    for z in range(2):
                        uv[pl.ds(base + 8 * z + 2 * i + m, 8, stride=16), :] = value[:, 128 * z : 128 * z + 128]
            return carry

        lax.fori_loop(0, 16, block, 0)
        for copy in copies:
            copy.wait()
        for t in range(4):
            pltpu.make_async_copy(f.at[:, t], f_out.at[:, t], f_sems.at[t]).wait()


def rim_kernel(idx, w, pot, out):
    for t in range(4):
        c, s = cos_sin(pot[t])
        for m in range(2):
            re, im = w[0, m, t], w[1, m, t]
            x = jnp.concatenate([c * re + s * im, c * im - s * re], axis=0)
            out[:, (2 * t + m) * NZ : (2 * t + m + 1) * NZ] = x


def halo_kernel(idx, halo, table, coef, uv_in, corr, uv):
    edge_uv = idx[6] * 128
    out = jnp.dot(table[idx[0]], halo[...], precision=lax.Precision.HIGHEST, preferred_element_type=f32)
    corr[...] = out
    k = coef[pl.ds(pl.multiple_of(idx[5] * 8, 8), 8), :]
    for m in range(2):
        cells = []
        for t in range(4):
            piece = out[:, (2 * t + m) * NZ : (2 * t + m + 1) * NZ]
            cells.append((piece[:8], piece[8:]))
        u, v = reduce_cells(cells, k)
        for i, value in enumerate((u[0], u[1], v[0], v[1])):
            for z in range(2):
                line = pl.ds(edge_uv + 8 * z + 2 * i + m, 8, stride=16)
                uv[line, :] = uv_in[line, :] + value[:, 128 * z : 128 * z + 128]


def row_swap(x, shift):
    return pltpu.roll(x, shift, 2)


def first_rows(core, shape):
    row = lax.broadcasted_iota(jnp.int32, shape, 2)
    return (lax.shift_right_logical(row, 2) ^ core) == 0


def tiles(x):
    return x.reshape(x.shape[0] // 16, 2, 8, 128)


def wide(x):
    x = tiles(x)
    rows = 8 * x.shape[0]
    return jnp.concatenate([x[:, z].reshape(rows, 128) for z in range(2)], axis=1)


def narrow(x):
    rows = x.shape[0] // 8
    return jnp.stack([x[:, 128 * z : 128 * z + 128].reshape(rows, 8, 128) for z in range(2)], axis=1)


def row_weights(chip):
    return chip[...].reshape(64, 1, 8, 128)


def pair_kernel(idx, own, received, chip, uv, m_out):
    a, b = tiles(own[...]), tiles(received[...])
    mask = first_rows(idx[1], a.shape)
    ends = jnp.where(mask, a, b)
    inner = jnp.where(mask, b, a)
    inner = inner + row_swap(inner, 4)
    k = row_weights(chip)
    out = ends + k[..., 0:1] * inner + k[..., 1:2] * row_swap(inner, 2)
    uv[...] = out.reshape(uv.shape)
    m_out[...] = inner.reshape(uv.shape)


def pair_axial_kernel(idx, m, chip, ah, al, out):
    x = wide(m[...])
    row = lax.broadcasted_iota(jnp.int32, (1, 1, 8, 128), 2)
    sign = jnp.where((row & 2) == 0, -1.0, 1.0)
    a = times(x, ah[0], al[0])
    b = a + times(x, ah[1], al[1])
    x = narrow(a) + sign * row_swap(narrow(b), 2)
    k = row_weights(chip)
    x = k[..., 2:3] * x + k[..., 3:4] * row_swap(x, 2)
    out[...] = x.reshape(out.shape)


def local_kernel(idx, f, coef, corr, *refs):
    sources, out, targets = refs[:5], refs[5], refs[6:11]
    g, sems = refs[11:]
    ah, al = targets[:2]
    copies = [
        pltpu.make_async_copy(x.at[idx[4]] if i == 4 else x, y, sems.at[i])
        for i, (x, y) in enumerate(zip(sources, targets))
    ]
    m, j = pl.program_id(0), pl.program_id(1)
    step = 2 * m + j

    @pl.when(step == 0)
    def _():
        for copy in copies:
            copy.start()

    g[...] = f[0]

    for side, row in ((0, 56), (1, 0)):

        @pl.when((idx[0] == side) & (j == 1 - side))
        def _():
            for t in range(4):
                at = pl.ds(pl.multiple_of((2 * t + m) * NZ, NZ), NZ)
                for c in range(2):
                    g[t, c, row : row + 8, :] += corr[8 * c : 8 * c + 8, at]

    k = coef[pl.ds(pl.multiple_of(j * 64, 64), 64), :]
    cells = [(g[t, 0], g[t, 1]) for t in range(4)]
    s, d = add(cells[1], cells[3]), sub(cells[1], cells[3])
    even = add(cmul(*weights(k, 4, NZ), s), cmul(*weights(k, 6, NZ), cells[2]))
    odd = cmul(*weights(k, 5, NZ), d)
    parts = [
        cmul(*weights(k, 3, NZ), cells[0]),
        add(even, odd),
        add(cmul(*weights(k, 6, NZ), s), cmul(*weights(k, 7, NZ), cells[2])),
        sub(even, odd),
    ]

    @pl.when(step == 0)
    def _():
        for copy in copies[:2]:
            copy.wait()

    re = jnp.concatenate([p[0] for p in parts], axis=0)
    im = jnp.concatenate([p[1] for p in parts], axis=0)
    re, im = complex_times(re, im, ah, al)
    for t in range(4):
        out[0, t, 0] = re[t * 64 : (t + 1) * 64]
        out[0, t, 1] = im[t * 64 : (t + 1) * 64]

    @pl.when(step == 3)
    def _():
        for copy in copies[2:]:
            copy.wait()


def middle_kernel(idx, x, fwd, inv, mid, ah, al, after, after_too, out):
    x = x[...].reshape(CHIPS, 2, 2, 8, 128)
    x = jnp.concatenate([x[:, r, z].reshape(256, 128) for r in range(2) for z in range(2)], axis=1)
    g = dot(fwd[...], stacked(x))
    k = mid[...].T
    rows = []
    for r in range(2):
        col = slice(r * NZ, (r + 1) * NZ)
        kr, ki = weights(k[:64], r, NZ)
        rows.append(cmul(kr, ki, (g[:64, col], g[64:, col])))
    re, im = complex_times(*[jnp.concatenate([p[c] for p in rows], axis=0) for c in range(2)], ah, al)
    h = jnp.concatenate([jnp.concatenate([x[64 * r : 64 * r + 64] for x in (re, im)], axis=0) for r in range(2)], axis=1)
    y = dot(inv[...], stacked(h))
    y = jnp.stack([y[:, 128 * i : 128 * i + 128].reshape(CHIPS, 8, 128) for i in range(4)], axis=1)
    out[...] = y.reshape(out.shape)


def fetch(row, w, cs, w_out, cs_out, sems):
    rows = pl.ds(pl.multiple_of(row, 64), 64)
    copies = [pltpu.make_async_copy(cs.at[:, :, rows, :], cs_out, sems.at[2])]
    for m in range(2):
        copies.append(pltpu.make_async_copy(w.at[m, :, :, rows, :], w_out.at[m], sems.at[m]))
    return copies


def spread_kernel(idx, y, mA, chip, w, cs, keep, send, w_out, cs_out, sems):
    copies = fetch(idx[1] * 64, w, cs, w_out, cs_out, sems)
    for copy in copies:
        copy.start()
    x = tiles(y[...])
    total = x + row_swap(x, 4)
    k = row_weights(chip)
    inner = k[..., 0:1] * total + k[..., 1:2] * row_swap(total, 2) + tiles(mA[...])
    mask = first_rows(idx[1], x.shape)
    keep[...] = jnp.where(mask, x, inner).reshape(keep.shape)
    send[...] = jnp.where(mask, inner, x).reshape(keep.shape)
    for copy in copies:
        copy.wait()


def finish_kernel(half, idx, w, cs, y, coef, out):
    j = pl.program_id(0)
    rows = out.shape[3]
    here = pl.ds(pl.multiple_of(j * rows, rows), rows)
    k = coef[pl.ds(pl.multiple_of((idx[1] ^ half) * 64 + j * rows, rows), rows), :]
    first = j * rows * 16
    for m in range(2):
        a = [
            jnp.concatenate([y[pl.ds(first + 8 * z + 2 * i + m, rows, stride=16), :] for z in range(2)], axis=1)
            for i in range(4)
        ]
        left, right = (a[0], a[1]), (a[2], a[3])
        s, d = add(left, right), sub(left, right)
        even = cmul(*weights(k, 0, NZ), s)
        odd = cmul(*weights(k, 1, NZ), d)
        parts = [left, add(even, odd), cmul(*weights(k, 2, NZ), s), sub(even, odd)]
        for t in range(4):
            re, im = w[m, t, 0, here, :] + parts[t][0], w[m, t, 1, here, :] + parts[t][1]
            c, sn = cs[0, t, here, :], cs[1, t, here, :]
            out[0, m, t] = c * re + sn * im
            out[1, m, t] = c * im - sn * re


def finish_own_kernel(idx, w, cs, y, coef, w_all, cs_all, out, w_out, cs_out, sems):
    copies = fetch((idx[1] ^ 1) * 64, w_all, cs_all, w_out, cs_out, sems)

    @pl.when(pl.program_id(0) == 0)
    def _():
        for copy in copies:
            copy.start()

    finish_kernel(0, idx, w, cs, y, coef, out)

    @pl.when(pl.program_id(0) == pl.num_programs(0) - 1)
    def _():
        for copy in copies:
            copy.wait()


def finish_other_kernel(idx, w, cs, y, coef, before, out):
    finish_kernel(1, idx, w, cs, y, coef, out)


def call(kernel, idx, args, in_specs, out_shape, out_specs, grid=(1,), scratch=(), aliases=None, flops=0, nbytes=0):
    return pl.pallas_call(
        kernel,
        out_shape=out_shape,
        grid_spec=pltpu.PrefetchScalarGridSpec(
            num_scalar_prefetch=1, grid=grid, in_specs=in_specs, out_specs=out_specs, scratch_shapes=scratch
        ),
        input_output_aliases=aliases or {},
        compiler_params=pltpu.CompilerParams(
            dimension_semantics=("arbitrary",) * len(grid), vmem_limit_bytes=24 << 20
        ),
        cost_estimate=pl.CostEstimate(flops=flops, bytes_accessed=nbytes, transcendentals=0),
        name=kernel.__name__,
    )(idx, *args)


def whole(shape):
    return pl.BlockSpec(shape, lambda *_: (0,) * len(shape))


VM = pl.BlockSpec(memory_space=pltpu.VMEM)
ANY = pl.BlockSpec(memory_space=pl.ANY)


def near(*arrays):
    return tuple(pltpu.with_memory_space_constraint(x, pltpu.VMEM) for x in arrays)


def far(*arrays):
    return tuple(pltpu.with_memory_space_constraint(x, pltpu.HBM) for x in arrays)


def body(wave, potential):
    t = tables()
    rad = lax.axis_index("rad")
    ang = lax.axis_index("ang")
    core = ang % 2
    chip = ang // 2
    lane = jnp.arange(8, dtype=jnp.int32)
    edge = jnp.where(rad == 0, 15, 0)
    edge_uv = ((edge // 8) ^ core) * 8 + edge % 8
    idx = jnp.zeros(8, jnp.int32)
    for i, v in enumerate((rad, core, chip, rad * 2 + core, rad * 64 + core * 32 + chip, edge, edge_uv)):
        idx = jnp.where(lane == i, v.astype(jnp.int32), idx)

    sds = pltpu.VMEM
    wave, potential = far(wave, potential)
    rim = call(
        rim_kernel,
        idx,
        (wave, potential),
        [
            pl.BlockSpec((2, 2, 4, 8, NZ), lambda a, i: (0, 0, 0, i[5], 0)),
            pl.BlockSpec((4, 8, NZ), lambda a, i: (0, i[5], 0)),
        ],
        sds((16, 8 * NZ), f32),
        VM,
    )
    halo = lax.ppermute(rim, "rad", [(0, 1), (1, 0)])
    field = pltpu.HBM((2, 4, 2, LR, NZ), f32)
    lines = sds((1024, 128), f32)
    names = ("halo", "chip", "cell", "ah", "al", "fwd", "inv", "mid")
    stored = far(*(t[k] for k in names))
    shapes = [x.shape[1:] if k in ("chip", "cell", "mid") else x.shape for k, x in zip(names, stored)]
    targets = tuple(sds(shape, x.dtype) for shape, x in zip(shapes, stored))
    f, cs, uv, halo_table, chip_table, cell = call(
        advance_kernel,
        idx,
        (wave, potential, *far(t["main"]), stored[2], *stored[:3]),
        [
            pl.BlockSpec((2, 2, 1, LR, NZ), lambda a, i: (0, 0, a, 0, 0)),
            pl.BlockSpec((1, LR, NZ), lambda a, i: (a, 0, 0)),
            pl.BlockSpec((1, 256, 768), lambda a, i: (i[0], 0, 0)),
            pl.BlockSpec((1, LR, 128), lambda a, i: (i[0], 0, 0)),
        ]
        + [ANY] * 3,
        (field, pltpu.HBM((2, 4, LR, NZ), f32), sds((2048, 128), f32)) + targets[:3],
        (ANY, pl.BlockSpec((2, 1, LR, NZ), lambda a, i: (0, a, 0, 0)), VM, VM, VM, VM),
        grid=(4,),
        scratch=(
            pltpu.VMEM((2, 4, 2, LR, NZ), f32),
            pltpu.SemaphoreType.DMA((3,)),
            pltpu.SemaphoreType.DMA((4,)),
        ),
        flops=1 << 30,
        nbytes=5 << 20,
    )
    corr, uv = call(
        halo_kernel,
        idx,
        near(halo, halo_table, cell, uv),
        [VM] * 4,
        (sds((16, 8 * NZ), f32), sds((2048, 128), f32)),
        (VM, VM),
        aliases={4: 1},
        flops=1 << 20,
        nbytes=1 << 20,
    )
    other = [(i, i ^ 1) for i in range(2 * CHIPS)]
    groups = [[2 * q + c for q in range(CHIPS)] for c in range(2)]
    exchange = functools.partial(
        lax.all_to_all, axis_name="ang", split_axis=0, concat_axis=0, tiled=True, axis_index_groups=groups
    )
    received = lax.ppermute(uv[1024:], "ang", other)
    UV, m = call(
        pair_kernel,
        idx,
        near(uv[:1024], received, chip_table),
        [VM] * 3,
        (lines, lines),
        (VM, VM),
        flops=1 << 20,
        nbytes=2 << 20,
    )
    x = exchange(UV)
    field_spec = pl.BlockSpec((1, 4, 2, 64, NZ), lambda m, j, i: (m, 0, 0, j, 0))
    w, ah, al, fwd, inv, mid = call(
        local_kernel,
        idx,
        (*far(f), *near(cell, corr), *stored[3:]),
        [field_spec, VM, VM] + [ANY] * 5,
        (field,) + targets[3:],
        (field_spec,) + (VM,) * 5,
        grid=(2, 2),
        scratch=(pltpu.VMEM((4, 2, 64, NZ), f32), pltpu.SemaphoreType.DMA((5,))),
        flops=3 << 30,
        nbytes=5 << 20,
    )
    mA = call(
        pair_axial_kernel,
        idx,
        near(m, chip_table, ah, al),
        [VM] * 4,
        lines,
        VM,
        flops=1 << 29,
        nbytes=2 << 20,
    )
    y = call(
        middle_kernel,
        idx,
        (*near(x, fwd, inv, mid, ah, al), *far(w), *near(mA)),
        [VM] * 6 + [ANY, VM],
        lines,
        VM,
        flops=1 << 29,
        nbytes=3 << 20,
    )
    y = exchange(y)
    near_half = (sds((2, 4, 2, 64, NZ), f32), sds((2, 4, 64, NZ), f32))
    keep, send, w_own, cs_own = call(
        spread_kernel,
        idx,
        (*near(y, mA, chip_table), *far(w, cs)),
        [VM] * 3 + [ANY] * 2,
        (lines, lines) + near_half,
        (VM,) * 4,
        scratch=(pltpu.SemaphoreType.DMA((3,)),),
        flops=1 << 20,
        nbytes=5 << 20,
    )
    received = lax.ppermute(send, "ang", other)
    size = 32

    def out_spec(half):
        return pl.BlockSpec(
            (2, 2, 4, size, NZ), lambda a, i: (0, 0, 0, (i[1] ^ half) * (64 // size) + a, 0)
        )

    out, w_other, cs_other = call(
        finish_own_kernel,
        idx,
        (*near(w_own, cs_own, keep, cell), *far(w, cs)),
        [VM] * 4 + [ANY] * 2,
        (pltpu.HBM(wave.shape, f32),) + near_half,
        (out_spec(0), VM, VM),
        grid=(64 // size,),
        scratch=(pltpu.SemaphoreType.DMA((3,)),),
        flops=1 << 22,
        nbytes=6 << 20,
    )
    return call(
        finish_other_kernel,
        idx,
        (*near(w_other, cs_other, received, cell), out),
        [VM] * 4 + [ANY],
        pltpu.HBM(wave.shape, f32),
        out_spec(1),
        grid=(64 // size,),
        aliases={5: 0},
        flops=1 << 22,
        nbytes=6 << 20,
    )


def solution(mesh):
    placed = (P(None, None, "ang", "rad", None), P("ang", "rad", None))
    return jax.shard_map(
        body,
        mesh=mesh,
        in_specs=placed,
        out_specs=P(None, None, "ang", "rad", None),
        check_vma=False,
    )
```

```python
import functools

import jax
import jax.numpy as jnp
import numpy as np
from jax import lax
from jax.experimental import pallas as pl
from jax.experimental.pallas import tpu as pltpu
from jax.sharding import PartitionSpec as P

NA = 256
NR = 256
NZ = 256
CHIPS = 32
LR = 128
f32 = jnp.float32
bf16 = jnp.bfloat16
UNROLL = 2


def split(a):
    hi = np.asarray(a, np.float32).astype(jnp.bfloat16)
    lo = (np.asarray(a, np.float64) - hi.astype(np.float64)).astype(np.float32)
    return hi, lo.astype(jnp.bfloat16)


def coefficients():
    j = np.arange(NR, dtype=np.float32)
    radius = np.float32(1.0) + np.float32(9.0) * (j + np.float32(0.5)) / np.float32(NR)
    return (np.float32(100000.0) / (radius * radius)).astype(np.float64)


def radial_tables():
    lap = np.zeros((NR, NR))
    for d, c in ((0, -30.0), (1, 16.0), (2, -1.0)):
        for j in range(NR - d):
            lap[j, j + d] = c / 12.0
            lap[j + d, j] = c / 12.0
    k = 0.25 * lap
    even = np.eye(NR) - k @ k / 2.0
    odd = -k + k @ k @ k / 6.0
    main, halo = [], []
    for side in range(2):
        own = slice(LR * side, LR * side + LR)
        a, b = even[own, own], odd[own, own]
        hi, lo = split(np.block([[a, -b], [b, a]]))
        main.append(np.concatenate([hi, hi, lo], axis=1))
        rows = slice(120, 128) if side == 0 else slice(128, 136)
        cols = slice(128, 136) if side == 0 else slice(120, 128)
        a, b = even[rows, cols], odd[rows, cols]
        halo.append(np.block([[a, -b], [b, a]]))
    return np.stack(main), np.stack(halo).astype(np.float32)


def axial_tables():
    n = np.arange(1, NZ + 1)
    sine = np.sqrt(2.0 / (NZ + 1)) * np.sin(np.pi * (n[:, None] * n[None, :]) / (NZ + 1))
    s = 1.5 * (2.0 - 2.0 * np.cos(np.pi * n / (NZ + 1)))
    gain = (1.0 - 1j * s) / (1.0 + 1j * s)
    full = (sine * gain[None, :]) @ sine
    re, im = full.real, full.imag
    return split(np.stack([re, im - re, re + im]))


def dirichlet(c, size):
    off = 0.1 - 1j * c
    mat = np.zeros((size, size), complex)
    for t in range(size):
        mat[t, t] = 1.0 + 2j * c
        if t:
            mat[t, t - 1] = off
            mat[t - 1, t] = off
    inv = np.linalg.inv(mat)
    return inv, -off * inv[:, 0]


def angle_tables():
    cell = np.zeros((2, LR, 128), np.float32)
    chip = np.zeros((2, 2, 4, 64, 1, 128), np.float32)
    mid = np.zeros((2, 2, 32, 1, 128), np.float32)
    angle = np.arange(NA)
    second = 2.0 * np.cos(2.0 * np.pi * angle / NA) - 2.0
    for g, c in enumerate(coefficients()):
        rho = 0.1 / (0.1 - 1j * c)
        scale = 2.4 * (1.0 - rho)
        inv, p = dirichlet(c, 3)
        w0 = 2.0 * rho - 1.0
        values = [
            (p[0] + p[2]) / 2,
            (p[0] - p[2]) / 2,
            p[1],
            w0,
            (w0 + scale * (inv[0, 0] + inv[0, 2])) / 2,
            (w0 + scale * (inv[0, 0] - inv[0, 2])) / 2,
            scale * inv[0, 1],
            w0 + scale * inv[1, 1],
        ]
        side, j = divmod(g, LR)
        for k, value in enumerate(values):
            cell[side, j, 2 * k] = value.real
            cell[side, j, 2 * k + 1] = value.imag
        inv8, p8 = dirichlet(c, 7)
        core, jj = divmod(j, 64)
        middle, local = p8[3], scale * inv8[3, 3]
        for k, value in enumerate((middle.real, middle.imag, local.real, local.imag)):
            chip[side, core, k, jj] = value
        symbol = 1.0 / (1.2 + (0.1 - 1j * c) * second)
        coarse = scale * symbol.reshape(8, CHIPS).sum(0) / 8.0
        pos, r = divmod(jj, 2)
        mid[side, core, pos, 0, 64 * r : 64 * r + 32] = coarse.real
        mid[side, core, pos, 0, 64 * r + 32 : 64 * r + 64] = coarse.imag
    return cell, chip.reshape(4, 4, 64, 1, 128), mid.reshape(128, 1, 128)


def fourier_tables():
    k = np.arange(CHIPS)
    q = np.arange(CHIPS)
    fwd = np.zeros((2, 2, CHIPS, CHIPS, 2, 2, 2))
    inv = np.zeros((CHIPS, 2, 2, 2, 2, 2, CHIPS))
    for n in range(2):
        phase = -2.0 * np.pi * ((k[:, None] * (q[None, :] + n)) % CHIPS) / CHIPS
        e = np.exp(1j * phase)
        for s in range(2):
            fwd[0, s, :, :, n, 0, s] = e.real
            fwd[0, s, :, :, n, 1, s] = -e.imag
            fwd[1, s, :, :, n, 0, s] = e.imag
            fwd[1, s, :, :, n, 1, s] = e.real
            d = np.conj(e).T / CHIPS
            inv[:, n, 0, s, 0, s, :] = d.real
            inv[:, n, 0, s, 1, s, :] = -d.imag
            inv[:, n, 1, s, 0, s, :] = d.imag
            inv[:, n, 1, s, 1, s, :] = d.real
    fwd = fwd.reshape(128, 256)
    inv = inv.reshape(256, 128)
    fh, fl = split(fwd)
    ih, il = split(inv)
    return np.stack([fh, fl]), np.stack([ih, il])


@functools.cache
def tables():
    main, halo = radial_tables()
    ah, al = axial_tables()
    cell, chip, mid = angle_tables()
    fwd, inv = fourier_tables()
    return dict(main=main, halo=halo, ah=ah, al=al, cell=cell, chip=chip, mid=mid, fwd=fwd, inv=inv)


def dot(a, b):
    return jnp.dot(a, b, preferred_element_type=f32)


def halves(x):
    hi = x.astype(bf16)
    return hi, (x - hi.astype(f32)).astype(bf16)


def stacked(x):
    hi, lo = halves(x)
    return jnp.concatenate([hi, lo, hi], axis=0)


def times(x, high, low):
    hi, lo = halves(x)
    rows = x.shape[0]
    both = dot(jnp.concatenate([hi, lo], axis=0), high[...])
    return both[:rows] + both[rows:] + dot(hi, low[...])


def apply(table, x):
    hi, lo = halves(x)
    rows = table.shape[1]
    both = dot(table[...].reshape(2 * rows, table.shape[2]), hi)
    return both[:rows] + both[rows:] + dot(table[0], lo)


def complex_times(re, im, high, low):
    p, q, r = [times(x, high.at[i], low.at[i]) for i, x in enumerate((re + im, re, im))]
    return p - r, p + q


SIN = (-0.16666657119790096, 0.008333017866982043, -0.00019806657092710876, 2.600148052222563e-06)
COS = (
    -0.4999999955093015,
    0.041666640791225444,
    -0.0013888404392796263,
    2.476193429595472e-05,
    -2.607799377413178e-07,
)


def cos_sin(x):
    y = 0.5 * x
    q = y * y
    a = jnp.full_like(q, SIN[-1])
    for c in SIN[-2::-1]:
        a = a * q + c
    b = jnp.full_like(q, COS[-1])
    for c in COS[-2::-1]:
        b = b * q + c
    s = y + y * (q * a)
    c = 1.0 + q * b
    s2 = s + s
    return 1.0 - s2 * s, s2 * c


def cmul(cr, ci, x):
    return (cr * x[0] - ci * x[1], cr * x[1] + ci * x[0])


def add(x, y):
    return (x[0] + y[0], x[1] + y[1])


def sub(x, y):
    return (x[0] - y[0], x[1] - y[1])


def weights(coef, k, width):
    shape = (coef.shape[0], width)
    return tuple(jnp.broadcast_to(coef[:, i : i + 1], shape) for i in (2 * k, 2 * k + 1))


def reduce_cells(f, coef):
    width = f[0][0].shape[-1]
    s, d = add(f[1], f[3]), sub(f[1], f[3])
    even = add(cmul(*weights(coef, 0, width), s), cmul(*weights(coef, 2, width), f[2]))
    odd = cmul(*weights(coef, 1, width), d)
    return add(add(f[0], even), odd), sub(even, odd)


def advance_kernel(idx, w, pot, main, *refs):
    sources, (f_out, cs_out, uv), targets = refs[:8], refs[8:11], refs[11:19]
    w_in, pot_in, main_in, f, cs, sems, in_sems, out_sems = refs[19:]
    own = {1: idx[3], 2: idx[0], 7: idx[4]}
    copies = [
        pltpu.make_async_copy(x.at[own[i]] if i in own else x, y, sems.at[i])
        for i, (x, y) in enumerate(zip(sources, targets))
    ]
    fetch_main = pltpu.make_async_copy(main.at[idx[0]], main_in, in_sems.at[8])
    fetches = [
        (
            pltpu.make_async_copy(pot.at[t], pot_in.at[t], in_sems.at[t]),
            pltpu.make_async_copy(w.at[:, :, t], w_in.at[:, :, t], in_sems.at[4 + t]),
        )
        for t in range(4)
    ]
    leaving = []
    for copy in fetches[0]:
        copy.start()
    fetch_main.start()
    for pair in fetches[1:]:
        for copy in pair:
            copy.start()
    for copy in copies:
        copy.start()
    for t in range(4):
        fetches[t][0].wait()
        c, s = cos_sin(pot_in[t])
        cs[0, t] = c
        cs[1, t] = s
        fetches[t][1].wait()
        if t == 0:
            fetch_main.wait()
        for m in range(2):
            re, im = w_in[0, m, t], w_in[1, m, t]
            x = jnp.concatenate([c * re + s * im, c * im - s * re], axis=0)
            f[m, t] = dot(main_in[...], stacked(x)).reshape(2, LR, NZ)
        for j in range(2):
            rows = pl.ds(64 * j, 64)
            for m in range(2):
                leaving.append((f.at[m, t, :, rows, :], f_out.at[m, j, t]))
            leaving.append((cs.at[:, t, rows, :], cs_out.at[j, :, t]))
        first = len(leaving) - 6
        for i in range(6):
            leaving[first + i] = pltpu.make_async_copy(*leaving[first + i], out_sems.at[first + i])
            leaving[first + i].start()
    for copy in copies:
        copy.wait()
    coef = targets[2]

    def block(b, carry):
        rows = pl.ds(pl.multiple_of(b * 8, 8), 8)
        base = (lax.shift_right_logical(b, 3) ^ idx[1]) * 1024 + (b & 7) * 128
        k = coef[rows, :]
        for m in range(2):
            u, v = reduce_cells([(f[m, t, 0, rows, :], f[m, t, 1, rows, :]) for t in range(4)], k)
            for i, value in enumerate((u[0], u[1], v[0], v[1])):
                for z in range(2):
                    uv[pl.ds(base + 8 * z + 2 * i + m, 8, stride=16), :] = value[:, 128 * z : 128 * z + 128]
        return carry

    lax.fori_loop(0, 16, block, 0, unroll=UNROLL)
    for copy in leaving:
        copy.wait()


def rim_kernel(idx, w, pot, out):
    for t in range(4):
        c, s = cos_sin(pot[t])
        for m in range(2):
            re, im = w[0, m, t], w[1, m, t]
            x = jnp.concatenate([c * re + s * im, c * im - s * re], axis=0)
            out[:, (2 * t + m) * NZ : (2 * t + m + 1) * NZ] = x


def halo_part(table, halo):
    return jnp.dot(table, halo, precision=lax.Precision.HIGHEST, preferred_element_type=f32)


def halo_kernel(idx, halo, table, coef, uv_in, uv):
    edge_uv = idx[6] * 128
    out = halo_part(table[idx[0]], halo[...])
    k = coef[pl.ds(pl.multiple_of(idx[5] * 8, 8), 8), :]
    for m in range(2):
        cells = []
        for t in range(4):
            piece = out[:, (2 * t + m) * NZ : (2 * t + m + 1) * NZ]
            cells.append((piece[:8], piece[8:]))
        u, v = reduce_cells(cells, k)
        for i, value in enumerate((u[0], u[1], v[0], v[1])):
            for z in range(2):
                line = pl.ds(edge_uv + 8 * z + 2 * i + m, 8, stride=16)
                uv[line, :] = uv_in[line, :] + value[:, 128 * z : 128 * z + 128]


def row_swap(x, shift):
    return pltpu.roll(x, shift, 2)


def first_rows(core, shape):
    row = lax.broadcasted_iota(jnp.int32, shape, 2)
    return (lax.shift_right_logical(row, 2) ^ core) == 0


def tiles(x):
    return x.reshape(x.shape[0] // 16, 2, 8, 128)


def wide(x):
    x = tiles(x)
    rows = 8 * x.shape[0]
    return jnp.concatenate([x[:, z].reshape(rows, 128) for z in range(2)], axis=1)


def narrow(x):
    rows = x.shape[0] // 8
    return jnp.stack([x[:, 128 * z : 128 * z + 128].reshape(rows, 8, 128) for z in range(2)], axis=1)


def row_times(chip, k, x):
    shape = (64, 1, 8, 128)
    re = jnp.broadcast_to(chip[k].reshape(64, 1, 1, 128), shape)
    im = jnp.broadcast_to(chip[k + 1].reshape(64, 1, 1, 128), shape) * part_sign()
    return re * x + im * row_swap(x, 2)


def part_sign():
    row = lax.broadcasted_iota(jnp.int32, (1, 1, 8, 128), 2)
    return jnp.where((row & 2) == 0, -1.0, 1.0)


def pair_kernel(idx, own, received, chip, uv, m_out):
    a, b = tiles(own[...]), tiles(received[...])
    mask = first_rows(idx[1], a.shape)
    ends = jnp.where(mask, a, b)
    inner = jnp.where(mask, b, a)
    inner = inner + row_swap(inner, 4)
    low = first_rows(0, (1, 1, 8, 128))
    m_out[...] = jnp.where(low, inner[:32], inner[32:]).reshape(512, 128)
    uv[...] = (ends + row_times(chip, 0, inner)).reshape(uv.shape)


def local_kernel(idx, f, halo_far, m_rows, *refs):
    sources, after, out, mA = refs[:5], refs[5], refs[6], refs[7]
    chip, cell, chip_local, ah, al, halo, halo_table, g, sems = refs[8:]
    tables = [
        pltpu.make_async_copy(sources[0].at[idx[0]], cell, sems.at[4]),
        pltpu.make_async_copy(sources[1].at[idx[3], pl.ds(0, 2)], chip, sems.at[5]),
        pltpu.make_async_copy(sources[1].at[idx[3], pl.ds(2, 2)], chip_local, sems.at[10]),
        pltpu.make_async_copy(sources[2], ah, sems.at[6]),
        pltpu.make_async_copy(sources[3], al, sems.at[7]),
        pltpu.make_async_copy(sources[4], halo_table, sems.at[8]),
        pltpu.make_async_copy(halo_far, halo, sems.at[9]),
    ]
    copies = [pltpu.make_async_copy(f.at[m, j], g.at[m, j], sems.at[2 * m + j]) for m in range(2) for j in range(2)]
    for copy in tables + copies:
        copy.start()
    for copy in tables:
        copy.wait()

    halo[...] = halo_part(halo_table[idx[0]], halo[...])

    x = wide(m_rows[...])
    a = times(x, ah.at[0], al.at[0])
    b = a + times(x, ah.at[1], al.at[1])
    b = narrow(b)
    b = jnp.where(part_sign() < 0, -row_swap(b, 6), row_swap(b, 2))
    x = narrow(a) + b
    other, low = row_swap(x, 4), first_rows(0, (1, 1, 8, 128))
    x = jnp.concatenate([jnp.where(low, x, other), jnp.where(low, other, x)], axis=0)
    mA[...] = row_times(chip_local, 0, x).reshape(mA.shape)

    for m in range(2):
        for j in range(2):
            copies[2 * m + j].wait()

            @pl.when(idx[0] == 1 - j)
            def _():
                row = 56 * j
                for t in range(4):
                    at = slice((2 * t + m) * NZ, (2 * t + m + 1) * NZ)
                    for c in range(2):
                        g[m, j, t, c, row : row + 8, :] += halo[8 * c : 8 * c + 8, at]

            k = cell[64 * j : 64 * j + 64, :]
            cells = [(g[m, j, t, 0], g[m, j, t, 1]) for t in range(4)]
            s, d = add(cells[1], cells[3]), sub(cells[1], cells[3])
            even = add(cmul(*weights(k, 4, NZ), s), cmul(*weights(k, 6, NZ), cells[2]))
            odd = cmul(*weights(k, 5, NZ), d)
            parts = [
                cmul(*weights(k, 3, NZ), cells[0]),
                add(even, odd),
                add(cmul(*weights(k, 6, NZ), s), cmul(*weights(k, 7, NZ), cells[2])),
                sub(even, odd),
            ]
            re = jnp.concatenate([p[0] for p in parts], axis=0)
            im = jnp.concatenate([p[1] for p in parts], axis=0)
            re, im = complex_times(re, im, ah, al)
            for t in range(4):
                out[m, t, 0, 64 * j : 64 * j + 64, :] = re[t * 64 : (t + 1) * 64]
                out[m, t, 1, 64 * j : 64 * j + 64, :] = im[t * 64 : (t + 1) * 64]


def middle_kernel(idx, x, fwd, inv, mid, ah, al, out, y, sems):
    x = x[...].reshape(CHIPS, 4, 8, 128)
    x = jnp.concatenate([x[:, i].reshape(256, 128) for i in range(4)], axis=1)
    g = apply(fwd, x)
    k = jnp.broadcast_to(mid[...], (8, 128)).T
    rows = []
    for r in range(2):
        col = slice(r * NZ, (r + 1) * NZ)
        kr, ki = [
            jnp.concatenate([jnp.broadcast_to(k[64 * r + 32 * c : 64 * r + 32 * c + 32, 0:1], (32, NZ))] * 2, axis=0)
            for c in range(2)
        ]
        rows.append(cmul(kr, ki, (g[:64, col], g[64:, col])))
    re, im = complex_times(*[jnp.concatenate([p[c] for p in rows], axis=0) for c in range(2)], ah, al)
    copies = []
    for r in range(2):
        h = jnp.concatenate([x[64 * r : 64 * r + 64] for x in (re, im)], axis=0)
        part = apply(inv, h)
        for z in range(2):
            y[:, 2 * r + z] = part[:, 128 * z : 128 * z + 128].reshape(CHIPS, 8, 128)
        lines = pl.ds(2 * r, 2)
        copies.append(pltpu.make_async_copy(y.at[:, lines], out.at[:, lines], sems.at[r]))
        copies[-1].start()
    for copy in copies:
        copy.wait()


def fetch(row, cs, cs_out, sem):
    return pltpu.make_async_copy(cs.at[row], cs_out, sem)


def spread_kernel(idx, y, mA, chip, after, cs, cell_far, keep, send, cs_own, cs_other, cell, sems):
    copies = [fetch(idx[1] ^ i, cs, x, sems.at[i]) for i, x in enumerate((cs_own, cs_other))]
    copies.append(pltpu.make_async_copy(cell_far.at[idx[0]], cell, sems.at[2]))
    for copy in copies:
        copy.start()
    x = tiles(y[...])
    total = x + row_swap(x, 4)
    inner = row_times(chip, 0, total) + tiles(mA[...])
    mask = first_rows(idx[1], x.shape)
    keep[...] = jnp.where(mask, x, inner).reshape(keep.shape)
    send[...] = jnp.where(mask, inner, x).reshape(keep.shape)
    for copy in copies:
        copy.wait()


CHUNK = 16


def finish_kernel(half, idx, w, cs, y, coef, out, o, sems):
    place = (idx[1] ^ half) * 64

    def leave(n):
        rows = pl.ds(pl.multiple_of(n * CHUNK, CHUNK), CHUNK)
        there = pl.ds(pl.multiple_of(place + n * CHUNK, CHUNK), CHUNK)
        return pltpu.make_async_copy(o.at[:, :, :, rows, :], out.at[:, :, :, there, :], sems.at[n])

    for n in range(64 // CHUNK):
        here = slice(n * CHUNK, (n + 1) * CHUNK)
        there = pl.ds(pl.multiple_of(place + n * CHUNK, CHUNK), CHUNK)
        k = coef[there, :]
        for m in range(2):
            a = [
                jnp.concatenate(
                    [y[pl.ds(n * CHUNK * 16 + 8 * z + 2 * i + m, CHUNK, stride=16), :] for z in range(2)], axis=1
                )
                for i in range(4)
            ]
            left, right = (a[0], a[1]), (a[2], a[3])
            s, d = add(left, right), sub(left, right)
            even = cmul(*weights(k, 0, NZ), s)
            odd = cmul(*weights(k, 1, NZ), d)
            parts = [left, add(even, odd), cmul(*weights(k, 2, NZ), s), sub(even, odd)]
            for t in range(4):
                re, im = w[m, t, 0, there, :] + parts[t][0], w[m, t, 1, there, :] + parts[t][1]
                c, sn = cs[0, t, here, :], cs[1, t, here, :]
                o[0, m, t, here, :] = c * re + sn * im
                o[1, m, t, here, :] = c * im - sn * re
        leave(n).start()
    for n in range(64 // CHUNK):
        leave(n).wait()


def finish_own_kernel(idx, w, cs, y, coef, out, o, sems):
    finish_kernel(0, idx, w, cs, y, coef, out, o, sems)


def finish_other_kernel(idx, w, cs, y, coef, before, out, o, sems):
    finish_kernel(1, idx, w, cs, y, coef, out, o, sems)


def call(kernel, idx, args, in_specs, out_shape, out_specs, grid=(1,), scratch=(), aliases=None, flops=0, nbytes=0):
    return pl.pallas_call(
        kernel,
        out_shape=out_shape,
        grid_spec=pltpu.PrefetchScalarGridSpec(
            num_scalar_prefetch=1, grid=grid, in_specs=in_specs, out_specs=out_specs, scratch_shapes=scratch
        ),
        input_output_aliases=aliases or {},
        compiler_params=pltpu.CompilerParams(
            dimension_semantics=("arbitrary",) * len(grid), vmem_limit_bytes=24 << 20
        ),
        cost_estimate=pl.CostEstimate(flops=flops, bytes_accessed=nbytes, transcendentals=0),
        name=kernel.__name__,
    )(idx, *args)


def whole(shape):
    return pl.BlockSpec(shape, lambda *_: (0,) * len(shape))


VM = pl.BlockSpec(memory_space=pltpu.VMEM)
ANY = pl.BlockSpec(memory_space=pl.ANY)


def near(*arrays):
    return tuple(pltpu.with_memory_space_constraint(x, pltpu.VMEM) for x in arrays)


def far(*arrays):
    return tuple(pltpu.with_memory_space_constraint(x, pltpu.HBM) for x in arrays)


def body(wave, potential):
    t = tables()
    rad = lax.axis_index("rad")
    ang = lax.axis_index("ang")
    core = ang % 2
    chip = ang // 2
    lane = jnp.arange(8, dtype=jnp.int32)
    edge = jnp.where(rad == 0, 15, 0)
    edge_uv = ((edge // 8) ^ core) * 8 + edge % 8
    idx = jnp.zeros(8, jnp.int32)
    for i, v in enumerate((rad, core, chip, rad * 2 + core, rad * 64 + core * 32 + chip, edge, edge_uv)):
        idx = jnp.where(lane == i, v.astype(jnp.int32), idx)

    sds = pltpu.VMEM
    wave, potential = far(wave, potential)
    rim = call(
        rim_kernel,
        idx,
        (wave, potential),
        [
            pl.BlockSpec((2, 2, 4, 8, NZ), lambda a, i: (0, 0, 0, i[5], 0)),
            pl.BlockSpec((4, 8, NZ), lambda a, i: (0, i[5], 0)),
        ],
        sds((16, 8 * NZ), f32),
        VM,
    )
    halo = lax.ppermute(rim, "rad", [(0, 1), (1, 0)])
    field = pltpu.HBM((2, 4, 2, LR, NZ), f32)
    lines = sds((1024, 128), f32)
    names = ("halo", "chip", "cell", "ah", "al", "fwd", "inv", "mid")
    stored = far(*(t[k] for k in names))
    shapes = [x.shape[1:] if k in ("chip", "cell", "mid") else x.shape for k, x in zip(names, stored)]
    targets = tuple(sds(shape, x.dtype) for shape, x in zip(shapes, stored))
    f, cs, uv, halo_table, chip_table, cell, ah, al, fwd, inv, mid = call(
        advance_kernel,
        idx,
        (wave, potential, *far(t["main"]), *stored),
        [ANY] * (3 + len(stored)),
        (
            pltpu.HBM((2, 2, 4, 2, 64, NZ), f32),
            pltpu.HBM((2, 2, 4, 64, NZ), f32),
            sds((2048, 128), f32),
        )
        + targets,
        (ANY, ANY, VM) + (VM,) * len(stored),
        scratch=(
            pltpu.VMEM((2, 2, 4, LR, NZ), f32),
            pltpu.VMEM((4, LR, NZ), f32),
            pltpu.VMEM((256, 768), bf16),
            pltpu.VMEM((2, 4, 2, LR, NZ), f32),
            pltpu.VMEM((2, 4, LR, NZ), f32),
            pltpu.SemaphoreType.DMA((len(stored),)),
            pltpu.SemaphoreType.DMA((9,)),
            pltpu.SemaphoreType.DMA((24,)),
        ),
        flops=1 << 30,
        nbytes=5 << 20,
    )
    uv = call(
        halo_kernel,
        idx,
        near(halo, halo_table, cell, uv),
        [VM] * 4,
        sds((2048, 128), f32),
        VM,
        aliases={4: 0},
        flops=1 << 20,
        nbytes=1 << 20,
    )
    other = [(i, i ^ 1) for i in range(2 * CHIPS)]
    groups = [[2 * q + c for q in range(CHIPS)] for c in range(2)]
    exchange = functools.partial(
        lax.all_to_all, axis_name="ang", split_axis=0, concat_axis=0, tiled=True, axis_index_groups=groups
    )
    received = lax.ppermute(uv[1024:], "ang", other)
    UV, m = call(
        pair_kernel,
        idx,
        near(uv[:1024], received, chip_table),
        [VM] * 3,
        (lines, sds((512, 128), f32)),
        (VM, VM),
        flops=1 << 20,
        nbytes=2 << 20,
    )
    x = exchange(UV)
    y = call(
        middle_kernel,
        idx,
        near(x, fwd, inv, mid, ah, al),
        [VM] * 6,
        pltpu.HBM((CHIPS, 4, 8, 128), f32),
        ANY,
        scratch=(pltpu.VMEM((CHIPS, 4, 8, 128), f32), pltpu.SemaphoreType.DMA((2,))),
        flops=1 << 29,
        nbytes=3 << 20,
    ).reshape(lines.shape)
    w, mA, chip_table = call(
        local_kernel,
        idx,
        (*far(f, halo), *near(m), *[stored[i] for i in (2, 1, 3, 4, 0)], *far(y)),
        [ANY, ANY, VM] + [ANY] * 6,
        (sds(field.shape, f32), lines, sds((2, 64, 1, 128), f32)),
        (VM,) * 3,
        scratch=(
            pltpu.VMEM((LR, 128), f32),
            pltpu.VMEM((2, 64, 1, 128), f32),
            pltpu.VMEM(stored[3].shape, bf16),
            pltpu.VMEM(stored[4].shape, bf16),
            pltpu.VMEM((16, 8 * NZ), f32),
            pltpu.VMEM((2, 16, 16), f32),
            pltpu.VMEM((2, 2, 4, 2, 64, NZ), f32),
            pltpu.SemaphoreType.DMA((11,)),
        ),
        flops=3 << 30,
        nbytes=5 << 20,
    )
    y = exchange(y)
    near_cs = sds((2, 4, 64, NZ), f32)
    keep, send, cs_own, cs_other, cell = call(
        spread_kernel,
        idx,
        (*near(y, mA, chip_table, w), *far(cs), stored[2]),
        [VM] * 4 + [ANY] * 2,
        (lines, lines, near_cs, near_cs, targets[2]),
        (VM,) * 5,
        scratch=(pltpu.SemaphoreType.DMA((3,)),),
        flops=1 << 20,
        nbytes=5 << 20,
    )
    received = lax.ppermute(send, "ang", other)
    scratch = (pltpu.VMEM((2, 2, 4, 64, NZ), f32), pltpu.SemaphoreType.DMA((64 // CHUNK,)))
    whole_out = pltpu.HBM(wave.shape, f32)
    work = dict(flops=1 << 22, nbytes=6 << 20)
    out = call(
        finish_own_kernel, idx, near(w, cs_own, keep, cell), [VM] * 4, whole_out, ANY, scratch=scratch, **work
    )
    return call(
        finish_other_kernel,
        idx,
        (*near(w, cs_other, received, cell), out),
        [VM] * 4 + [ANY],
        whole_out,
        ANY,
        scratch=scratch,
        aliases={5: 0},
        **work,
    )


def solution(mesh):
    placed = (P(None, None, "ang", "rad", None), P("ang", "rad", None))
    return jax.shard_map(
        body,
        mesh=mesh,
        in_specs=placed,
        out_specs=P(None, None, "ang", "rad", None),
        check_vma=False,
    )
```

```python
import functools

import jax
import jax.numpy as jnp
import numpy as np
from jax import lax
from jax.experimental import pallas as pl
from jax.experimental.pallas import tpu as pltpu
from jax.sharding import PartitionSpec as P

NA = 256
NR = 256
NZ = 256
CHIPS = 32
LR = 128
f32 = jnp.float32
bf16 = jnp.bfloat16
UNROLL = 2


def split(a):
    hi = np.asarray(a, np.float32).astype(jnp.bfloat16)
    lo = (np.asarray(a, np.float64) - hi.astype(np.float64)).astype(np.float32)
    return hi, lo.astype(jnp.bfloat16)


def coefficients():
    j = np.arange(NR, dtype=np.float32)
    radius = np.float32(1.0) + np.float32(9.0) * (j + np.float32(0.5)) / np.float32(NR)
    return (np.float32(100000.0) / (radius * radius)).astype(np.float64)


def radial_tables():
    lap = np.zeros((NR, NR))
    for d, c in ((0, -30.0), (1, 16.0), (2, -1.0)):
        for j in range(NR - d):
            lap[j, j + d] = c / 12.0
            lap[j + d, j] = c / 12.0
    k = 0.25 * lap
    even = np.eye(NR) - k @ k / 2.0
    odd = -k + k @ k @ k / 6.0
    main, halo = [], []
    for side in range(2):
        own = slice(LR * side, LR * side + LR)
        a, b = even[own, own], odd[own, own]
        hi, lo = split(np.block([[a, -b], [b, a]]))
        main.append(np.concatenate([hi, hi, lo], axis=1))
        rows = slice(120, 128) if side == 0 else slice(128, 136)
        cols = slice(128, 136) if side == 0 else slice(120, 128)
        a, b = even[rows, cols], odd[rows, cols]
        halo.append(np.block([[a, -b], [b, a]]))
    return np.stack(main), np.stack(halo).astype(np.float32)


def axial_tables():
    n = np.arange(1, NZ + 1)
    sine = np.sqrt(2.0 / (NZ + 1)) * np.sin(np.pi * (n[:, None] * n[None, :]) / (NZ + 1))
    s = 1.5 * (2.0 - 2.0 * np.cos(np.pi * n / (NZ + 1)))
    gain = (1.0 - 1j * s) / (1.0 + 1j * s)
    full = (sine * gain[None, :]) @ sine
    re, im = full.real, full.imag
    return split(np.stack([re, im - re, re + im]))


def dirichlet(c, size):
    off = 0.1 - 1j * c
    mat = np.zeros((size, size), complex)
    for t in range(size):
        mat[t, t] = 1.0 + 2j * c
        if t:
            mat[t, t - 1] = off
            mat[t - 1, t] = off
    inv = np.linalg.inv(mat)
    return inv, -off * inv[:, 0]


def angle_tables():
    cell = np.zeros((2, LR, 128), np.float32)
    chip = np.zeros((2, 2, 4, 64, 1, 128), np.float32)
    mid = np.zeros((2, 2, 32, 1, 128), np.float32)
    angle = np.arange(NA)
    second = 2.0 * np.cos(2.0 * np.pi * angle / NA) - 2.0
    for g, c in enumerate(coefficients()):
        rho = 0.1 / (0.1 - 1j * c)
        scale = 2.4 * (1.0 - rho)
        inv, p = dirichlet(c, 3)
        w0 = 2.0 * rho - 1.0
        values = [
            (p[0] + p[2]) / 2,
            (p[0] - p[2]) / 2,
            p[1],
            w0,
            (w0 + scale * (inv[0, 0] + inv[0, 2])) / 2,
            (w0 + scale * (inv[0, 0] - inv[0, 2])) / 2,
            scale * inv[0, 1],
            w0 + scale * inv[1, 1],
        ]
        side, j = divmod(g, LR)
        for k, value in enumerate(values):
            cell[side, j, 2 * k] = value.real
            cell[side, j, 2 * k + 1] = value.imag
        inv8, p8 = dirichlet(c, 7)
        core, jj = divmod(j, 64)
        middle, local = p8[3], scale * inv8[3, 3]
        for k, value in enumerate((middle.real, middle.imag, local.real, local.imag)):
            chip[side, core, k, jj] = value
        symbol = 1.0 / (1.2 + (0.1 - 1j * c) * second)
        coarse = scale * symbol.reshape(8, CHIPS).sum(0) / 8.0
        pos, r = divmod(jj, 2)
        mid[side, core, pos, 0, 64 * r : 64 * r + 32] = coarse.real
        mid[side, core, pos, 0, 64 * r + 32 : 64 * r + 64] = coarse.imag
    return cell, chip.reshape(4, 4, 64, 1, 128), mid.reshape(128, 1, 128)


def fourier_tables():
    k = np.arange(CHIPS)
    q = np.arange(CHIPS)
    fwd = np.zeros((2, 2, CHIPS, CHIPS, 2, 2, 2))
    inv = np.zeros((CHIPS, 2, 2, 2, 2, 2, CHIPS))
    for n in range(2):
        phase = -2.0 * np.pi * ((k[:, None] * (q[None, :] + n)) % CHIPS) / CHIPS
        e = np.exp(1j * phase)
        for s in range(2):
            fwd[0, s, :, :, n, 0, s] = e.real
            fwd[0, s, :, :, n, 1, s] = -e.imag
            fwd[1, s, :, :, n, 0, s] = e.imag
            fwd[1, s, :, :, n, 1, s] = e.real
            d = np.conj(e).T / CHIPS
            inv[:, n, 0, s, 0, s, :] = d.real
            inv[:, n, 0, s, 1, s, :] = -d.imag
            inv[:, n, 1, s, 0, s, :] = d.imag
            inv[:, n, 1, s, 1, s, :] = d.real
    fwd = fwd.reshape(128, 256)
    inv = inv.reshape(256, 128)
    fh, fl = split(fwd)
    ih, il = split(inv)
    return np.stack([fh, fl]), np.stack([ih, il])


@functools.cache
def tables():
    main, halo = radial_tables()
    ah, al = axial_tables()
    cell, chip, mid = angle_tables()
    fwd, inv = fourier_tables()
    return dict(main=main, halo=halo, ah=ah, al=al, cell=cell, chip=chip, mid=mid, fwd=fwd, inv=inv)


def dot(a, b):
    return jnp.dot(a, b, preferred_element_type=f32)


def halves(x):
    hi = x.astype(bf16)
    return hi, (x - hi.astype(f32)).astype(bf16)


def stacked(x):
    hi, lo = halves(x)
    return jnp.concatenate([hi, lo, hi], axis=0)


def times(x, high, low):
    hi, lo = halves(x)
    rows = x.shape[0]
    both = dot(jnp.concatenate([hi, lo], axis=0), high[...])
    return both[:rows] + both[rows:] + dot(hi, low[...])


def apply(table, x):
    hi, lo = halves(x)
    rows = table.shape[1]
    both = dot(table[...].reshape(2 * rows, table.shape[2]), hi)
    return both[:rows] + both[rows:] + dot(table[0], lo)


def complex_times(re, im, high, low):
    p, q, r = [times(x, high.at[i], low.at[i]) for i, x in enumerate((re + im, re, im))]
    return p - r, p + q


SIN = (-0.16666657119790096, 0.008333017866982043, -0.00019806657092710876, 2.600148052222563e-06)
COS = (
    -0.4999999955093015,
    0.041666640791225444,
    -0.0013888404392796263,
    2.476193429595472e-05,
    -2.607799377413178e-07,
)


def cos_sin(x):
    y = 0.5 * x
    q = y * y
    a = jnp.full_like(q, SIN[-1])
    for c in SIN[-2::-1]:
        a = a * q + c
    b = jnp.full_like(q, COS[-1])
    for c in COS[-2::-1]:
        b = b * q + c
    s = y + y * (q * a)
    c = 1.0 + q * b
    s2 = s + s
    return 1.0 - s2 * s, s2 * c


def cmul(cr, ci, x):
    return (cr * x[0] - ci * x[1], cr * x[1] + ci * x[0])


def add(x, y):
    return (x[0] + y[0], x[1] + y[1])


def sub(x, y):
    return (x[0] - y[0], x[1] - y[1])


def weights(coef, k, width):
    shape = (coef.shape[0], width)
    return tuple(jnp.broadcast_to(coef[:, i : i + 1], shape) for i in (2 * k, 2 * k + 1))


def reduce_cells(f, coef):
    width = f[0][0].shape[-1]
    s, d = add(f[1], f[3]), sub(f[1], f[3])
    even = add(cmul(*weights(coef, 0, width), s), cmul(*weights(coef, 2, width), f[2]))
    odd = cmul(*weights(coef, 1, width), d)
    return add(add(f[0], even), odd), sub(even, odd)


def advance_kernel(idx, w, pot, w0, pot0, main_in, *refs):
    sources, (f_out, cs_out, uv), targets = refs[:8], refs[8:11], refs[11:19]
    w_in, pot_in, f, cs, staged, sems, in_sems, out_sems = refs[19:]
    own = {1: idx[3], 2: idx[0], 7: idx[4]}
    copies = [
        pltpu.make_async_copy(x.at[own[i]] if i in own else x, y, sems.at[i])
        for i, (x, y) in enumerate(zip(sources, targets))
    ]
    fetches = [
        (
            pltpu.make_async_copy(pot.at[t], pot_in.at[t], in_sems.at[t]),
            pltpu.make_async_copy(w.at[:, :, t], w_in.at[:, :, t], in_sems.at[4 + t]),
        )
        for t in range(4)
    ]
    leaving = []
    for pair in fetches[1:]:
        for copy in pair:
            copy.start()
    for copy in copies:
        copy.start()

    def rotate(t):
        for row in range(0, LR, 16):
            rows, imag = slice(row, row + 16), slice(LR + row, LR + row + 16)
            c, s = cos_sin(pot_in[t, rows, :] if t else pot0[rows, :])
            cs[0, t, rows, :] = c
            cs[1, t, rows, :] = s
            for m in range(2):
                re, im = [w_in[i, m, t, rows, :] if t else w0[i, m, rows, :] for i in range(2)]
                for at, x in ((rows, c * re + s * im), (imag, c * im - s * re)):
                    staged[t % 2, m, 0, at, :], staged[t % 2, m, 1, at, :] = halves(x)

    def multiply(t):
        for m in range(2):
            hi, lo = staged[t % 2, m, 0], staged[t % 2, m, 1]
            x = jnp.concatenate([hi, lo, hi], axis=0)
            f[m, t] = dot(main_in[...], x).reshape(2, LR, NZ)

    for t in range(5):
        if 0 < t < 4:
            for copy in fetches[t]:
                copy.wait()
        if t > 0:
            multiply(t - 1)
        if t < 4:
            rotate(t)
        if t == 0:
            continue
        for j in range(2):
            rows = pl.ds(64 * j, 64)
            for m in range(2):
                leaving.append((f.at[m, t - 1, :, rows, :], f_out.at[m, j, t - 1]))
            leaving.append((cs.at[:, t - 1, rows, :], cs_out.at[j, :, t - 1]))
        first = len(leaving) - 6
        for i in range(6):
            leaving[first + i] = pltpu.make_async_copy(*leaving[first + i], out_sems.at[first + i])
            leaving[first + i].start()
    for copy in copies:
        copy.wait()
    coef = targets[2]

    def block(b, carry):
        rows = pl.ds(pl.multiple_of(b * 8, 8), 8)
        base = (lax.shift_right_logical(b, 3) ^ idx[1]) * 1024 + (b & 7) * 128
        k = coef[rows, :]
        for m in range(2):
            u, v = reduce_cells([(f[m, t, 0, rows, :], f[m, t, 1, rows, :]) for t in range(4)], k)
            for i, value in enumerate((u[0], u[1], v[0], v[1])):
                for z in range(2):
                    uv[pl.ds(base + 8 * z + 2 * i + m, 8, stride=16), :] = value[:, 128 * z : 128 * z + 128]
        return carry

    lax.fori_loop(0, 16, block, 0, unroll=UNROLL)
    for copy in leaving:
        copy.wait()


def rim_kernel(idx, w, pot, main, out, w0, pot0, main_in, w_rim, pot_rim, sems):
    rows = pl.ds(pl.multiple_of(idx[5] * 8, 8), 8)
    pairs = (
        (pot.at[:, rows, :], pot_rim),
        (w.at[:, :, :, rows, :], w_rim),
        (pot.at[0], pot0),
        (w.at[:, :, 0], w0),
        (main.at[idx[0]], main_in),
    )
    copies = [pltpu.make_async_copy(a, b, sems.at[i]) for i, (a, b) in enumerate(pairs)]
    for copy in copies:
        copy.start()
    for copy in copies[:2]:
        copy.wait()
    for t in range(4):
        c, s = cos_sin(pot_rim[t])
        for m in range(2):
            re, im = w_rim[0, m, t], w_rim[1, m, t]
            x = jnp.concatenate([c * re + s * im, c * im - s * re], axis=0)
            out[:, (2 * t + m) * NZ : (2 * t + m + 1) * NZ] = x
    for copy in copies[2:]:
        copy.wait()


def halo_part(table, halo):
    return jnp.dot(table, halo, precision=lax.Precision.HIGHEST, preferred_element_type=f32)


def halo_kernel(idx, halo, table, coef, uv_in, uv):
    edge_uv = idx[6] * 128
    out = halo_part(table[idx[0]], halo[...])
    k = coef[pl.ds(pl.multiple_of(idx[5] * 8, 8), 8), :]
    for m in range(2):
        cells = []
        for t in range(4):
            piece = out[:, (2 * t + m) * NZ : (2 * t + m + 1) * NZ]
            cells.append((piece[:8], piece[8:]))
        u, v = reduce_cells(cells, k)
        for i, value in enumerate((u[0], u[1], v[0], v[1])):
            for z in range(2):
                line = pl.ds(edge_uv + 8 * z + 2 * i + m, 8, stride=16)
                uv[line, :] = uv_in[line, :] + value[:, 128 * z : 128 * z + 128]


def row_swap(x, shift):
    return pltpu.roll(x, shift, 2)


def first_rows(core, shape):
    row = lax.broadcasted_iota(jnp.int32, shape, 2)
    return (lax.shift_right_logical(row, 2) ^ core) == 0


def tiles(x):
    return x.reshape(x.shape[0] // 16, 2, 8, 128)


def wide(x):
    x = tiles(x)
    rows = 8 * x.shape[0]
    return jnp.concatenate([x[:, z].reshape(rows, 128) for z in range(2)], axis=1)


def narrow(x):
    rows = x.shape[0] // 8
    return jnp.stack([x[:, 128 * z : 128 * z + 128].reshape(rows, 8, 128) for z in range(2)], axis=1)


def row_times(chip, k, x):
    shape = (64, 1, 8, 128)
    re = jnp.broadcast_to(chip[k].reshape(64, 1, 1, 128), shape)
    im = jnp.broadcast_to(chip[k + 1].reshape(64, 1, 1, 128), shape) * part_sign()
    return re * x + im * row_swap(x, 2)


def part_sign():
    row = lax.broadcasted_iota(jnp.int32, (1, 1, 8, 128), 2)
    return jnp.where((row & 2) == 0, -1.0, 1.0)


def pair_kernel(idx, own, received, chip, uv, m_out):
    a, b = tiles(own[...]), tiles(received[...])
    mask = first_rows(idx[1], a.shape)
    ends = jnp.where(mask, a, b)
    inner = jnp.where(mask, b, a)
    inner = inner + row_swap(inner, 4)
    low = first_rows(0, (1, 1, 8, 128))
    m_out[...] = jnp.where(low, inner[:32], inner[32:]).reshape(512, 128)
    uv[...] = (ends + row_times(chip, 0, inner)).reshape(uv.shape)


def local_kernel(idx, f, halo_far, m_rows, *refs):
    sources, after, out, mA = refs[:5], refs[5], refs[6], refs[7]
    chip, cell, chip_local, ah, al, halo, halo_table, g, sems = refs[8:]
    tables = [
        pltpu.make_async_copy(sources[0].at[idx[0]], cell, sems.at[4]),
        pltpu.make_async_copy(sources[1].at[idx[3], pl.ds(0, 2)], chip, sems.at[5]),
        pltpu.make_async_copy(sources[1].at[idx[3], pl.ds(2, 2)], chip_local, sems.at[10]),
        pltpu.make_async_copy(sources[2], ah, sems.at[6]),
        pltpu.make_async_copy(sources[3], al, sems.at[7]),
        pltpu.make_async_copy(sources[4], halo_table, sems.at[8]),
        pltpu.make_async_copy(halo_far, halo, sems.at[9]),
    ]
    copies = [pltpu.make_async_copy(f.at[m, j], g.at[m, j], sems.at[2 * m + j]) for m in range(2) for j in range(2)]
    for copy in tables + copies:
        copy.start()
    for copy in tables:
        copy.wait()

    halo[...] = halo_part(halo_table[idx[0]], halo[...])

    x = wide(m_rows[...])
    a = times(x, ah.at[0], al.at[0])
    b = a + times(x, ah.at[1], al.at[1])
    b = narrow(b)
    b = jnp.where(part_sign() < 0, -row_swap(b, 6), row_swap(b, 2))
    x = narrow(a) + b
    other, low = row_swap(x, 4), first_rows(0, (1, 1, 8, 128))
    x = jnp.concatenate([jnp.where(low, x, other), jnp.where(low, other, x)], axis=0)
    mA[...] = row_times(chip_local, 0, x).reshape(mA.shape)

    for m in range(2):
        for j in range(2):
            copies[2 * m + j].wait()

            @pl.when(idx[0] == 1 - j)
            def _():
                row = 56 * j
                for t in range(4):
                    at = slice((2 * t + m) * NZ, (2 * t + m + 1) * NZ)
                    for c in range(2):
                        g[m, j, t, c, row : row + 8, :] += halo[8 * c : 8 * c + 8, at]

            k = cell[64 * j : 64 * j + 64, :]
            cells = [(g[m, j, t, 0], g[m, j, t, 1]) for t in range(4)]
            s, d = add(cells[1], cells[3]), sub(cells[1], cells[3])
            even = add(cmul(*weights(k, 4, NZ), s), cmul(*weights(k, 6, NZ), cells[2]))
            odd = cmul(*weights(k, 5, NZ), d)
            parts = [
                cmul(*weights(k, 3, NZ), cells[0]),
                add(even, odd),
                add(cmul(*weights(k, 6, NZ), s), cmul(*weights(k, 7, NZ), cells[2])),
                sub(even, odd),
            ]
            re = jnp.concatenate([p[0] for p in parts], axis=0)
            im = jnp.concatenate([p[1] for p in parts], axis=0)
            re, im = complex_times(re, im, ah, al)
            for t in range(4):
                out[m, t, 0, 64 * j : 64 * j + 64, :] = re[t * 64 : (t + 1) * 64]
                out[m, t, 1, 64 * j : 64 * j + 64, :] = im[t * 64 : (t + 1) * 64]


def middle_kernel(idx, x, fwd, inv, mid, ah, al, out, y, sems):
    x = x[...].reshape(CHIPS, 4, 8, 128)
    x = jnp.concatenate([x[:, i].reshape(256, 128) for i in range(4)], axis=1)
    g = apply(fwd, x)
    k = jnp.broadcast_to(mid[...], (8, 128)).T
    rows = []
    for r in range(2):
        col = slice(r * NZ, (r + 1) * NZ)
        kr, ki = [
            jnp.concatenate([jnp.broadcast_to(k[64 * r + 32 * c : 64 * r + 32 * c + 32, 0:1], (32, NZ))] * 2, axis=0)
            for c in range(2)
        ]
        rows.append(cmul(kr, ki, (g[:64, col], g[64:, col])))
    re, im = complex_times(*[jnp.concatenate([p[c] for p in rows], axis=0) for c in range(2)], ah, al)
    copies = []
    for r in range(2):
        h = jnp.concatenate([x[64 * r : 64 * r + 64] for x in (re, im)], axis=0)
        part = apply(inv, h)
        for z in range(2):
            y[:, 2 * r + z] = part[:, 128 * z : 128 * z + 128].reshape(CHIPS, 8, 128)
        lines = pl.ds(2 * r, 2)
        copies.append(pltpu.make_async_copy(y.at[:, lines], out.at[:, lines], sems.at[r]))
        copies[-1].start()
    for copy in copies:
        copy.wait()


def fetch(row, cs, cs_out, sem):
    return pltpu.make_async_copy(cs.at[row], cs_out, sem)


def spread_kernel(idx, y, mA, chip, after, cs, cell_far, keep, send, cs_own, cs_other, cell, sems):
    copies = [fetch(idx[1] ^ i, cs, x, sems.at[i]) for i, x in enumerate((cs_own, cs_other))]
    copies.append(pltpu.make_async_copy(cell_far.at[idx[0]], cell, sems.at[2]))
    for copy in copies:
        copy.start()
    x = tiles(y[...])
    total = x + row_swap(x, 4)
    inner = row_times(chip, 0, total) + tiles(mA[...])
    mask = first_rows(idx[1], x.shape)
    keep[...] = jnp.where(mask, x, inner).reshape(keep.shape)
    send[...] = jnp.where(mask, inner, x).reshape(keep.shape)
    for copy in copies:
        copy.wait()


CHUNK = 16


def finish_kernel(half, idx, w, cs, y, coef, out, o, sems):
    place = (idx[1] ^ half) * 64

    def leave(n):
        rows = pl.ds(pl.multiple_of(n * CHUNK, CHUNK), CHUNK)
        there = pl.ds(pl.multiple_of(place + n * CHUNK, CHUNK), CHUNK)
        return pltpu.make_async_copy(o.at[:, :, :, rows, :], out.at[:, :, :, there, :], sems.at[n])

    for n in range(64 // CHUNK):
        here = slice(n * CHUNK, (n + 1) * CHUNK)
        there = pl.ds(pl.multiple_of(place + n * CHUNK, CHUNK), CHUNK)
        k = coef[there, :]
        for m in range(2):
            a = [
                jnp.concatenate(
                    [y[pl.ds(n * CHUNK * 16 + 8 * z + 2 * i + m, CHUNK, stride=16), :] for z in range(2)], axis=1
                )
                for i in range(4)
            ]
            left, right = (a[0], a[1]), (a[2], a[3])
            s, d = add(left, right), sub(left, right)
            even = cmul(*weights(k, 0, NZ), s)
            odd = cmul(*weights(k, 1, NZ), d)
            parts = [left, add(even, odd), cmul(*weights(k, 2, NZ), s), sub(even, odd)]
            for t in range(4):
                re, im = w[m, t, 0, there, :] + parts[t][0], w[m, t, 1, there, :] + parts[t][1]
                c, sn = cs[0, t, here, :], cs[1, t, here, :]
                o[0, m, t, here, :] = c * re + sn * im
                o[1, m, t, here, :] = c * im - sn * re
        leave(n).start()
    for n in range(64 // CHUNK):
        leave(n).wait()


def finish_own_kernel(idx, w, cs, y, coef, out, o, sems):
    finish_kernel(0, idx, w, cs, y, coef, out, o, sems)


def finish_other_kernel(idx, w, cs, y, coef, before, out, o, sems):
    finish_kernel(1, idx, w, cs, y, coef, out, o, sems)


def call(kernel, idx, args, in_specs, out_shape, out_specs, grid=(1,), scratch=(), aliases=None, flops=0, nbytes=0):
    return pl.pallas_call(
        kernel,
        out_shape=out_shape,
        grid_spec=pltpu.PrefetchScalarGridSpec(
            num_scalar_prefetch=1, grid=grid, in_specs=in_specs, out_specs=out_specs, scratch_shapes=scratch
        ),
        input_output_aliases=aliases or {},
        compiler_params=pltpu.CompilerParams(
            dimension_semantics=("arbitrary",) * len(grid), vmem_limit_bytes=24 << 20
        ),
        cost_estimate=pl.CostEstimate(flops=flops, bytes_accessed=nbytes, transcendentals=0),
        name=kernel.__name__,
    )(idx, *args)


def whole(shape):
    return pl.BlockSpec(shape, lambda *_: (0,) * len(shape))


VM = pl.BlockSpec(memory_space=pltpu.VMEM)
ANY = pl.BlockSpec(memory_space=pl.ANY)


def near(*arrays):
    return tuple(pltpu.with_memory_space_constraint(x, pltpu.VMEM) for x in arrays)


def far(*arrays):
    return tuple(pltpu.with_memory_space_constraint(x, pltpu.HBM) for x in arrays)


def body(wave, potential):
    t = tables()
    rad = lax.axis_index("rad")
    ang = lax.axis_index("ang")
    core = ang % 2
    chip = ang // 2
    lane = jnp.arange(8, dtype=jnp.int32)
    edge = jnp.where(rad == 0, 15, 0)
    edge_uv = ((edge // 8) ^ core) * 8 + edge % 8
    idx = jnp.zeros(8, jnp.int32)
    for i, v in enumerate((rad, core, chip, rad * 2 + core, rad * 64 + core * 32 + chip, edge, edge_uv)):
        idx = jnp.where(lane == i, v.astype(jnp.int32), idx)

    sds = pltpu.VMEM
    wave, potential = far(wave, potential)
    rim, w0, pot0, main = call(
        rim_kernel,
        idx,
        (wave, potential, *far(t["main"])),
        [ANY] * 3,
        (sds((16, 8 * NZ), f32), sds((2, 2, LR, NZ), f32), sds((LR, NZ), f32), sds((256, 768), bf16)),
        (VM,) * 4,
        scratch=(
            pltpu.VMEM((2, 2, 4, 8, NZ), f32),
            pltpu.VMEM((4, 8, NZ), f32),
            pltpu.SemaphoreType.DMA((5,)),
        ),
    )
    halo = lax.ppermute(rim, "rad", [(0, 1), (1, 0)])
    field = pltpu.HBM((2, 4, 2, LR, NZ), f32)
    lines = sds((1024, 128), f32)
    names = ("halo", "chip", "cell", "ah", "al", "fwd", "inv", "mid")
    stored = far(*(t[k] for k in names))
    shapes = [x.shape[1:] if k in ("chip", "cell", "mid") else x.shape for k, x in zip(names, stored)]
    targets = tuple(sds(shape, x.dtype) for shape, x in zip(shapes, stored))
    f, cs, uv, halo_table, chip_table, cell, ah, al, fwd, inv, mid = call(
        advance_kernel,
        idx,
        (wave, potential, *near(w0, pot0, main), *stored),
        [ANY] * 2 + [VM] * 3 + [ANY] * len(stored),
        (
            pltpu.HBM((2, 2, 4, 2, 64, NZ), f32),
            pltpu.HBM((2, 2, 4, 64, NZ), f32),
            sds((2048, 128), f32),
        )
        + targets,
        (ANY, ANY, VM) + (VM,) * len(stored),
        scratch=(
            pltpu.VMEM((2, 2, 4, LR, NZ), f32),
            pltpu.VMEM((4, LR, NZ), f32),
            pltpu.VMEM((2, 4, 2, LR, NZ), f32),
            pltpu.VMEM((2, 4, LR, NZ), f32),
            pltpu.VMEM((2, 2, 2, 256, NZ), bf16),
            pltpu.SemaphoreType.DMA((len(stored),)),
            pltpu.SemaphoreType.DMA((9,)),
            pltpu.SemaphoreType.DMA((24,)),
        ),
        flops=1 << 30,
        nbytes=5 << 20,
    )
    uv = call(
        halo_kernel,
        idx,
        near(halo, halo_table, cell, uv),
        [VM] * 4,
        sds((2048, 128), f32),
        VM,
        aliases={4: 0},
        flops=1 << 20,
        nbytes=1 << 20,
    )
    other = [(i, i ^ 1) for i in range(2 * CHIPS)]
    groups = [[2 * q + c for q in range(CHIPS)] for c in range(2)]
    exchange = functools.partial(
        lax.all_to_all, axis_name="ang", split_axis=0, concat_axis=0, tiled=True, axis_index_groups=groups
    )
    received = lax.ppermute(uv[1024:], "ang", other)
    UV, m = call(
        pair_kernel,
        idx,
        near(uv[:1024], received, chip_table),
        [VM] * 3,
        (lines, sds((512, 128), f32)),
        (VM, VM),
        flops=1 << 20,
        nbytes=2 << 20,
    )
    x = exchange(UV)
    y = call(
        middle_kernel,
        idx,
        near(x, fwd, inv, mid, ah, al),
        [VM] * 6,
        pltpu.HBM((CHIPS, 4, 8, 128), f32),
        ANY,
        scratch=(pltpu.VMEM((CHIPS, 4, 8, 128), f32), pltpu.SemaphoreType.DMA((2,))),
        flops=1 << 29,
        nbytes=3 << 20,
    ).reshape(lines.shape)
    w, mA, chip_table = call(
        local_kernel,
        idx,
        (*far(f, halo), *near(m), *[stored[i] for i in (2, 1, 3, 4, 0)], *far(y)),
        [ANY, ANY, VM] + [ANY] * 6,
        (sds(field.shape, f32), lines, sds((2, 64, 1, 128), f32)),
        (VM,) * 3,
        scratch=(
            pltpu.VMEM((LR, 128), f32),
            pltpu.VMEM((2, 64, 1, 128), f32),
            pltpu.VMEM(stored[3].shape, bf16),
            pltpu.VMEM(stored[4].shape, bf16),
            pltpu.VMEM((16, 8 * NZ), f32),
            pltpu.VMEM((2, 16, 16), f32),
            pltpu.VMEM((2, 2, 4, 2, 64, NZ), f32),
            pltpu.SemaphoreType.DMA((11,)),
        ),
        flops=3 << 30,
        nbytes=5 << 20,
    )
    y = exchange(y)
    near_cs = sds((2, 4, 64, NZ), f32)
    keep, send, cs_own, cs_other, cell = call(
        spread_kernel,
        idx,
        (*near(y, mA, chip_table, w), *far(cs), stored[2]),
        [VM] * 4 + [ANY] * 2,
        (lines, lines, near_cs, near_cs, targets[2]),
        (VM,) * 5,
        scratch=(pltpu.SemaphoreType.DMA((3,)),),
        flops=1 << 20,
        nbytes=5 << 20,
    )
    received = lax.ppermute(send, "ang", other)
    scratch = (pltpu.VMEM((2, 2, 4, 64, NZ), f32), pltpu.SemaphoreType.DMA((64 // CHUNK,)))
    whole_out = pltpu.HBM(wave.shape, f32)
    work = dict(flops=1 << 22, nbytes=6 << 20)
    out = call(
        finish_own_kernel, idx, near(w, cs_own, keep, cell), [VM] * 4, whole_out, ANY, scratch=scratch, **work
    )
    return call(
        finish_other_kernel,
        idx,
        (*near(w, cs_other, received, cell), out),
        [VM] * 4 + [ANY],
        whole_out,
        ANY,
        scratch=scratch,
        aliases={5: 0},
        **work,
    )


def solution(mesh):
    placed = (P(None, None, "ang", "rad", None), P("ang", "rad", None))
    return jax.shard_map(
        body,
        mesh=mesh,
        in_specs=placed,
        out_specs=P(None, None, "ang", "rad", None),
        check_vma=False,
    )
```

```python
import functools

import jax
import jax.numpy as jnp
import numpy as np
from jax import lax
from jax.experimental import pallas as pl
from jax.experimental.pallas import tpu as pltpu
from jax.sharding import PartitionSpec as P

NA = 256
NR = 256
NZ = 256
CHIPS = 32
LR = 128
f32 = jnp.float32
bf16 = jnp.bfloat16
UNROLL = 2


def split(a):
    hi = np.asarray(a, np.float32).astype(jnp.bfloat16)
    lo = (np.asarray(a, np.float64) - hi.astype(np.float64)).astype(np.float32)
    return hi, lo.astype(jnp.bfloat16)


def coefficients():
    j = np.arange(NR, dtype=np.float32)
    radius = np.float32(1.0) + np.float32(9.0) * (j + np.float32(0.5)) / np.float32(NR)
    return (np.float32(100000.0) / (radius * radius)).astype(np.float64)


def radial_tables():
    lap = np.zeros((NR, NR))
    for d, c in ((0, -30.0), (1, 16.0), (2, -1.0)):
        for j in range(NR - d):
            lap[j, j + d] = c / 12.0
            lap[j + d, j] = c / 12.0
    k = 0.25 * lap
    even = np.eye(NR) - k @ k / 2.0
    odd = -k + k @ k @ k / 6.0
    main, halo = [], []
    for side in range(2):
        own = slice(LR * side, LR * side + LR)
        a, b = even[own, own], odd[own, own]
        hi, lo = split(np.block([[a, -b], [b, a]]))
        main.append(np.concatenate([hi, hi, lo], axis=1))
        rows = slice(120, 128) if side == 0 else slice(128, 136)
        cols = slice(128, 136) if side == 0 else slice(120, 128)
        a, b = even[rows, cols], odd[rows, cols]
        halo.append(np.block([[a, -b], [b, a]]))
    return np.stack(main), np.stack(halo).astype(np.float32)


def axial_tables():
    n = np.arange(1, NZ + 1)
    sine = np.sqrt(2.0 / (NZ + 1)) * np.sin(np.pi * (n[:, None] * n[None, :]) / (NZ + 1))
    s = 1.5 * (2.0 - 2.0 * np.cos(np.pi * n / (NZ + 1)))
    gain = (1.0 - 1j * s) / (1.0 + 1j * s)
    full = (sine * gain[None, :]) @ sine
    re, im = full.real, full.imag
    return split(np.stack([re, im - re, re + im]))


def dirichlet(c, size):
    off = 0.1 - 1j * c
    mat = np.zeros((size, size), complex)
    for t in range(size):
        mat[t, t] = 1.0 + 2j * c
        if t:
            mat[t, t - 1] = off
            mat[t - 1, t] = off
    inv = np.linalg.inv(mat)
    return inv, -off * inv[:, 0]


def angle_tables():
    cell = np.zeros((2, LR, 128), np.float32)
    chip = np.zeros((2, 2, 4, 64, 1, 128), np.float32)
    mid = np.zeros((2, 2, 32, 1, 128), np.float32)
    angle = np.arange(NA)
    second = 2.0 * np.cos(2.0 * np.pi * angle / NA) - 2.0
    for g, c in enumerate(coefficients()):
        rho = 0.1 / (0.1 - 1j * c)
        scale = 2.4 * (1.0 - rho)
        inv, p = dirichlet(c, 3)
        w0 = 2.0 * rho - 1.0
        values = [
            (p[0] + p[2]) / 2,
            (p[0] - p[2]) / 2,
            p[1],
            w0,
            (w0 + scale * (inv[0, 0] + inv[0, 2])) / 2,
            (w0 + scale * (inv[0, 0] - inv[0, 2])) / 2,
            scale * inv[0, 1],
            w0 + scale * inv[1, 1],
        ]
        side, j = divmod(g, LR)
        for k, value in enumerate(values):
            cell[side, j, 2 * k] = value.real
            cell[side, j, 2 * k + 1] = value.imag
        inv8, p8 = dirichlet(c, 7)
        core, jj = divmod(j, 64)
        middle, local = p8[3], scale * inv8[3, 3]
        for k, value in enumerate((middle.real, middle.imag, local.real, local.imag)):
            chip[side, core, k, jj] = value
        symbol = 1.0 / (1.2 + (0.1 - 1j * c) * second)
        coarse = scale * symbol.reshape(8, CHIPS).sum(0) / 8.0
        pos, r = divmod(jj, 2)
        mid[side, core, pos, 0, 64 * r : 64 * r + 32] = coarse.real
        mid[side, core, pos, 0, 64 * r + 32 : 64 * r + 64] = coarse.imag
    return cell, chip.reshape(4, 4, 64, 1, 128), mid.reshape(128, 1, 128)


def fourier_tables():
    k = np.arange(CHIPS)
    q = np.arange(CHIPS)
    fwd = np.zeros((2, 2, CHIPS, CHIPS, 2, 2, 2))
    inv = np.zeros((CHIPS, 2, 2, 2, 2, 2, CHIPS))
    for n in range(2):
        phase = -2.0 * np.pi * ((k[:, None] * (q[None, :] + n)) % CHIPS) / CHIPS
        e = np.exp(1j * phase)
        for s in range(2):
            fwd[0, s, :, :, n, 0, s] = e.real
            fwd[0, s, :, :, n, 1, s] = -e.imag
            fwd[1, s, :, :, n, 0, s] = e.imag
            fwd[1, s, :, :, n, 1, s] = e.real
            d = np.conj(e).T / CHIPS
            inv[:, n, 0, s, 0, s, :] = d.real
            inv[:, n, 0, s, 1, s, :] = -d.imag
            inv[:, n, 1, s, 0, s, :] = d.imag
            inv[:, n, 1, s, 1, s, :] = d.real
    fwd = fwd.reshape(128, 256)
    inv = inv.reshape(256, 128)
    fh, fl = split(fwd)
    ih, il = split(inv)
    return np.stack([fh, fl]), np.stack([ih, il])


@functools.cache
def tables():
    main, halo = radial_tables()
    ah, al = axial_tables()
    cell, chip, mid = angle_tables()
    fwd, inv = fourier_tables()
    return dict(main=main, halo=halo, ah=ah, al=al, cell=cell, chip=chip, mid=mid, fwd=fwd, inv=inv)


def dot(a, b):
    return jnp.dot(a, b, preferred_element_type=f32)


def halves(x):
    hi = x.astype(bf16)
    return hi, (x - hi.astype(f32)).astype(bf16)


def stacked(x):
    hi, lo = halves(x)
    return jnp.concatenate([hi, lo, hi], axis=0)


def times(x, high, low):
    hi, lo = halves(x)
    rows = x.shape[0]
    both = dot(jnp.concatenate([hi, lo], axis=0), high[...])
    return both[:rows] + both[rows:] + dot(hi, low[...])


def apply(table, x):
    hi, lo = halves(x)
    rows = table.shape[1]
    both = dot(table[...].reshape(2 * rows, table.shape[2]), hi)
    return both[:rows] + both[rows:] + dot(table[0], lo)


def complex_times(re, im, high, low):
    p, q, r = [times(x, high.at[i], low.at[i]) for i, x in enumerate((re + im, re, im))]
    return p - r, p + q


SIN = (-0.16666657119790096, 0.008333017866982043, -0.00019806657092710876, 2.600148052222563e-06)
COS = (
    -0.4999999955093015,
    0.041666640791225444,
    -0.0013888404392796263,
    2.476193429595472e-05,
    -2.607799377413178e-07,
)


def cos_sin(x):
    y = 0.5 * x
    q = y * y
    a = jnp.full_like(q, SIN[-1])
    for c in SIN[-2::-1]:
        a = a * q + c
    b = jnp.full_like(q, COS[-1])
    for c in COS[-2::-1]:
        b = b * q + c
    s = y + y * (q * a)
    c = 1.0 + q * b
    s2 = s + s
    return 1.0 - s2 * s, s2 * c


def cmul(cr, ci, x):
    return (cr * x[0] - ci * x[1], cr * x[1] + ci * x[0])


def add(x, y):
    return (x[0] + y[0], x[1] + y[1])


def sub(x, y):
    return (x[0] - y[0], x[1] - y[1])


def weights(coef, k, width):
    shape = (coef.shape[0], width)
    return tuple(jnp.broadcast_to(coef[:, i : i + 1], shape) for i in (2 * k, 2 * k + 1))


def reduce_cells(f, coef):
    width = f[0][0].shape[-1]
    s, d = add(f[1], f[3]), sub(f[1], f[3])
    even = add(cmul(*weights(coef, 0, width), s), cmul(*weights(coef, 2, width), f[2]))
    odd = cmul(*weights(coef, 1, width), d)
    return add(add(f[0], even), odd), sub(even, odd)


def advance_kernel(idx, w, pot, main, *refs):
    sources, (f_out, cs_out, uv), targets = refs[:8], refs[8:11], refs[11:19]
    w_in, pot_in, main_in, f, cs, staged, sems, in_sems, out_sems = refs[19:]
    own = {1: idx[3], 2: idx[0], 7: idx[4]}
    copies = [
        pltpu.make_async_copy(x.at[own[i]] if i in own else x, y, sems.at[i])
        for i, (x, y) in enumerate(zip(sources, targets))
    ]
    fetch_main = pltpu.make_async_copy(main.at[idx[0]], main_in, in_sems.at[8])
    fetches = [
        (
            pltpu.make_async_copy(pot.at[t], pot_in.at[t], in_sems.at[t]),
            pltpu.make_async_copy(w.at[:, :, t], w_in.at[:, :, t], in_sems.at[4 + t]),
        )
        for t in range(4)
    ]
    leaving = []
    for copy in fetches[0]:
        copy.start()
    fetch_main.start()
    for pair in fetches[1:]:
        for copy in pair:
            copy.start()
    for copy in copies:
        copy.start()

    def rotate(t):
        for row in range(0, LR, 16):
            rows, imag = slice(row, row + 16), slice(LR + row, LR + row + 16)
            c, s = cos_sin(pot_in[t, rows, :])
            cs[0, t, rows, :] = c
            cs[1, t, rows, :] = s
            for m in range(2):
                re, im = w_in[0, m, t, rows, :], w_in[1, m, t, rows, :]
                for at, x in ((rows, c * re + s * im), (imag, c * im - s * re)):
                    staged[t % 2, m, 0, at, :], staged[t % 2, m, 1, at, :] = halves(x)

    def multiply(t):
        for m in range(2):
            hi, lo = staged[t % 2, m, 0], staged[t % 2, m, 1]
            x = jnp.concatenate([hi, lo, hi], axis=0)
            f[m, t] = dot(main_in[...], x).reshape(2, LR, NZ)

    for t in range(5):
        if t < 4:
            for copy in fetches[t]:
                copy.wait()
        if t == 1:
            fetch_main.wait()
        if t > 0:
            multiply(t - 1)
        if t < 4:
            rotate(t)
        if t == 0:
            continue
        for j in range(2):
            rows = pl.ds(64 * j, 64)
            for m in range(2):
                leaving.append((f.at[m, t - 1, :, rows, :], f_out.at[m, j, t - 1]))
            leaving.append((cs.at[:, t - 1, rows, :], cs_out.at[j, :, t - 1]))
        first = len(leaving) - 6
        for i in range(6):
            leaving[first + i] = pltpu.make_async_copy(*leaving[first + i], out_sems.at[first + i])
            leaving[first + i].start()
    for copy in copies:
        copy.wait()
    coef = targets[2]

    def block(b, carry):
        rows = pl.ds(pl.multiple_of(b * 8, 8), 8)
        base = (lax.shift_right_logical(b, 3) ^ idx[1]) * 1024 + (b & 7) * 128
        k = coef[rows, :]
        for m in range(2):
            u, v = reduce_cells([(f[m, t, 0, rows, :], f[m, t, 1, rows, :]) for t in range(4)], k)
            for i, value in enumerate((u[0], u[1], v[0], v[1])):
                for z in range(2):
                    uv[pl.ds(base + 8 * z + 2 * i + m, 8, stride=16), :] = value[:, 128 * z : 128 * z + 128]
        return carry

    lax.fori_loop(0, 16, block, 0, unroll=UNROLL)
    for copy in leaving:
        copy.wait()


def rim_kernel(idx, w, pot, out):
    for t in range(4):
        c, s = cos_sin(pot[t])
        for m in range(2):
            re, im = w[0, m, t], w[1, m, t]
            x = jnp.concatenate([c * re + s * im, c * im - s * re], axis=0)
            out[:, (2 * t + m) * NZ : (2 * t + m + 1) * NZ] = x


def halo_part(table, halo):
    return jnp.dot(table, halo, precision=lax.Precision.HIGHEST, preferred_element_type=f32)


def halo_kernel(idx, halo, table, coef, uv_in, uv):
    edge_uv = idx[6] * 128
    out = halo_part(table[idx[0]], halo[...])
    k = coef[pl.ds(pl.multiple_of(idx[5] * 8, 8), 8), :]
    for m in range(2):
        cells = []
        for t in range(4):
            piece = out[:, (2 * t + m) * NZ : (2 * t + m + 1) * NZ]
            cells.append((piece[:8], piece[8:]))
        u, v = reduce_cells(cells, k)
        for i, value in enumerate((u[0], u[1], v[0], v[1])):
            for z in range(2):
                line = pl.ds(edge_uv + 8 * z + 2 * i + m, 8, stride=16)
                uv[line, :] = uv_in[line, :] + value[:, 128 * z : 128 * z + 128]


def row_swap(x, shift):
    return pltpu.roll(x, shift, 2)


def first_rows(core, shape):
    row = lax.broadcasted_iota(jnp.int32, shape, 2)
    return (lax.shift_right_logical(row, 2) ^ core) == 0


def tiles(x):
    return x.reshape(x.shape[0] // 16, 2, 8, 128)


def wide(x):
    x = tiles(x)
    rows = 8 * x.shape[0]
    return jnp.concatenate([x[:, z].reshape(rows, 128) for z in range(2)], axis=1)


def narrow(x):
    rows = x.shape[0] // 8
    return jnp.stack([x[:, 128 * z : 128 * z + 128].reshape(rows, 8, 128) for z in range(2)], axis=1)


def row_times(chip, k, x):
    shape = (64, 1, 8, 128)
    re = jnp.broadcast_to(chip[k].reshape(64, 1, 1, 128), shape)
    im = jnp.broadcast_to(chip[k + 1].reshape(64, 1, 1, 128), shape) * part_sign()
    return re * x + im * row_swap(x, 2)


def part_sign():
    row = lax.broadcasted_iota(jnp.int32, (1, 1, 8, 128), 2)
    return jnp.where((row & 2) == 0, -1.0, 1.0)


def pair_kernel(idx, own, received, chip, uv, m_out):
    a, b = tiles(own[...]), tiles(received[...])
    mask = first_rows(idx[1], a.shape)
    ends = jnp.where(mask, a, b)
    inner = jnp.where(mask, b, a)
    inner = inner + row_swap(inner, 4)
    low = first_rows(0, (1, 1, 8, 128))
    m_out[...] = jnp.where(low, inner[:32], inner[32:]).reshape(512, 128)
    uv[...] = (ends + row_times(chip, 0, inner)).reshape(uv.shape)


def local_kernel(idx, f, halo_far, m_rows, *refs):
    sources, after, out, mA = refs[:5], refs[5], refs[6], refs[7]
    chip, cell, chip_local, ah, al, halo, halo_table, g, sems = refs[8:]
    tables = [
        pltpu.make_async_copy(sources[0].at[idx[0]], cell, sems.at[4]),
        pltpu.make_async_copy(sources[1].at[idx[3], pl.ds(0, 2)], chip, sems.at[5]),
        pltpu.make_async_copy(sources[1].at[idx[3], pl.ds(2, 2)], chip_local, sems.at[10]),
        pltpu.make_async_copy(sources[2], ah, sems.at[6]),
        pltpu.make_async_copy(sources[3], al, sems.at[7]),
        pltpu.make_async_copy(sources[4], halo_table, sems.at[8]),
        pltpu.make_async_copy(halo_far, halo, sems.at[9]),
    ]
    copies = [pltpu.make_async_copy(f.at[m, j], g.at[m, j], sems.at[2 * m + j]) for m in range(2) for j in range(2)]
    for copy in tables + copies:
        copy.start()
    for copy in tables:
        copy.wait()

    halo[...] = halo_part(halo_table[idx[0]], halo[...])

    x = wide(m_rows[...])
    a = times(x, ah.at[0], al.at[0])
    b = a + times(x, ah.at[1], al.at[1])
    b = narrow(b)
    b = jnp.where(part_sign() < 0, -row_swap(b, 6), row_swap(b, 2))
    x = narrow(a) + b
    other, low = row_swap(x, 4), first_rows(0, (1, 1, 8, 128))
    x = jnp.concatenate([jnp.where(low, x, other), jnp.where(low, other, x)], axis=0)
    mA[...] = row_times(chip_local, 0, x).reshape(mA.shape)

    for m in range(2):
        for j in range(2):
            copies[2 * m + j].wait()

            @pl.when(idx[0] == 1 - j)
            def _():
                row = 56 * j
                for t in range(4):
                    at = slice((2 * t + m) * NZ, (2 * t + m + 1) * NZ)
                    for c in range(2):
                        g[m, j, t, c, row : row + 8, :] += halo[8 * c : 8 * c + 8, at]

            k = cell[64 * j : 64 * j + 64, :]
            cells = [(g[m, j, t, 0], g[m, j, t, 1]) for t in range(4)]
            s, d = add(cells[1], cells[3]), sub(cells[1], cells[3])
            even = add(cmul(*weights(k, 4, NZ), s), cmul(*weights(k, 6, NZ), cells[2]))
            odd = cmul(*weights(k, 5, NZ), d)
            parts = [
                cmul(*weights(k, 3, NZ), cells[0]),
                add(even, odd),
                add(cmul(*weights(k, 6, NZ), s), cmul(*weights(k, 7, NZ), cells[2])),
                sub(even, odd),
            ]
            re = jnp.concatenate([p[0] for p in parts], axis=0)
            im = jnp.concatenate([p[1] for p in parts], axis=0)
            re, im = complex_times(re, im, ah, al)
            for t in range(4):
                out[m, t, 0, 64 * j : 64 * j + 64, :] = re[t * 64 : (t + 1) * 64]
                out[m, t, 1, 64 * j : 64 * j + 64, :] = im[t * 64 : (t + 1) * 64]


def middle_kernel(idx, x, fwd, inv, mid, ah, al, out, y, sems):
    x = x[...].reshape(CHIPS, 4, 8, 128)
    x = jnp.concatenate([x[:, i].reshape(256, 128) for i in range(4)], axis=1)
    g = apply(fwd, x)
    k = jnp.broadcast_to(mid[...], (8, 128)).T
    rows = []
    for r in range(2):
        col = slice(r * NZ, (r + 1) * NZ)
        kr, ki = [
            jnp.concatenate([jnp.broadcast_to(k[64 * r + 32 * c : 64 * r + 32 * c + 32, 0:1], (32, NZ))] * 2, axis=0)
            for c in range(2)
        ]
        rows.append(cmul(kr, ki, (g[:64, col], g[64:, col])))
    re, im = complex_times(*[jnp.concatenate([p[c] for p in rows], axis=0) for c in range(2)], ah, al)
    copies = []
    for r in range(2):
        h = jnp.concatenate([x[64 * r : 64 * r + 64] for x in (re, im)], axis=0)
        part = apply(inv, h)
        for z in range(2):
            y[:, 2 * r + z] = part[:, 128 * z : 128 * z + 128].reshape(CHIPS, 8, 128)
        lines = pl.ds(2 * r, 2)
        copies.append(pltpu.make_async_copy(y.at[:, lines], out.at[:, lines], sems.at[r]))
        copies[-1].start()
    for copy in copies:
        copy.wait()


def fetch(row, cs, cs_out, sem):
    return pltpu.make_async_copy(cs.at[row], cs_out, sem)


def spread_kernel(idx, y, mA, chip, after, keep, send):
    x = tiles(y[...])
    total = x + row_swap(x, 4)
    inner = row_times(chip, 0, total) + tiles(mA[...])
    mask = first_rows(idx[1], x.shape)
    keep[...] = jnp.where(mask, x, inner).reshape(keep.shape)
    send[...] = jnp.where(mask, inner, x).reshape(keep.shape)


CHUNK = 16


CHUNK = 16


def gather_half(half, idx, w, y, coef, n):
    there = pl.ds(pl.multiple_of((idx[1] ^ half) * 64 + n * CHUNK, CHUNK), CHUNK)
    k = coef[there, :]
    for m in range(2):
        a = [
            jnp.concatenate(
                [y[pl.ds(n * CHUNK * 16 + 8 * z + 2 * i + m, CHUNK, stride=16), :] for z in range(2)], axis=1
            )
            for i in range(4)
        ]
        left, right = (a[0], a[1]), (a[2], a[3])
        s, d = add(left, right), sub(left, right)
        even = cmul(*weights(k, 0, NZ), s)
        odd = cmul(*weights(k, 1, NZ), d)
        parts = [left, add(even, odd), cmul(*weights(k, 2, NZ), s), sub(even, odd)]
        for t in range(4):
            yield m, t, w[m, t, 0, there, :] + parts[t][0], w[m, t, 1, there, :] + parts[t][1]


def rotate_out(o, cs, m, t, rows, re, im):
    c, s = cs[0, t, rows, :], cs[1, t, rows, :]
    o[0, m, t, rows, :] = c * re + s * im
    o[1, m, t, rows, :] = c * im - s * re


def leave(half, idx, o, out, sems, n):
    rows = pl.ds(n * CHUNK, CHUNK)
    there = pl.ds(pl.multiple_of((idx[1] ^ half) * 64 + n * CHUNK, CHUNK), CHUNK)
    return pltpu.make_async_copy(o.at[:, :, :, rows, :], out.at[:, :, :, there, :], sems.at[n])


def finish_own_kernel(idx, w, y, cell_far, cs_far, out, cs_other, cell, o, cs_own, sems, more):
    near_cell = pltpu.make_async_copy(cell_far.at[idx[0]], cell, more.at[2])
    near_cell.start()
    copies = [fetch(idx[1] ^ i, cs_far, x, more.at[i]) for i, x in enumerate((cs_own, cs_other))]
    for copy in copies:
        copy.start()
    near_cell.wait()
    for n in range(64 // CHUNK):
        rows = slice(n * CHUNK, (n + 1) * CHUNK)
        for m, t, re, im in gather_half(0, idx, w, y, cell, n):
            o[0, m, t, rows, :] = re
            o[1, m, t, rows, :] = im
    copies[0].wait()
    for n in range(64 // CHUNK):
        rows = slice(n * CHUNK, (n + 1) * CHUNK)
        for m in range(2):
            for t in range(4):
                rotate_out(o, cs_own, m, t, rows, o[0, m, t, rows, :], o[1, m, t, rows, :])
        leave(0, idx, o, out, sems, n).start()
    for n in range(64 // CHUNK):
        leave(0, idx, o, out, sems, n).wait()
    copies[1].wait()


def finish_other_kernel(idx, w, cs, y, coef, before, out, o, sems):
    for n in range(64 // CHUNK):
        rows = slice(n * CHUNK, (n + 1) * CHUNK)
        for m, t, re, im in gather_half(1, idx, w, y, coef, n):
            rotate_out(o, cs, m, t, rows, re, im)
        leave(1, idx, o, out, sems, n).start()
    for n in range(64 // CHUNK):
        leave(1, idx, o, out, sems, n).wait()


def call(kernel, idx, args, in_specs, out_shape, out_specs, grid=(1,), scratch=(), aliases=None, flops=0, nbytes=0):
    return pl.pallas_call(
        kernel,
        out_shape=out_shape,
        grid_spec=pltpu.PrefetchScalarGridSpec(
            num_scalar_prefetch=1, grid=grid, in_specs=in_specs, out_specs=out_specs, scratch_shapes=scratch
        ),
        input_output_aliases=aliases or {},
        compiler_params=pltpu.CompilerParams(
            dimension_semantics=("arbitrary",) * len(grid), vmem_limit_bytes=24 << 20
        ),
        cost_estimate=pl.CostEstimate(flops=flops, bytes_accessed=nbytes, transcendentals=0),
        name=kernel.__name__,
    )(idx, *args)


def whole(shape):
    return pl.BlockSpec(shape, lambda *_: (0,) * len(shape))


VM = pl.BlockSpec(memory_space=pltpu.VMEM)
ANY = pl.BlockSpec(memory_space=pl.ANY)


def near(*arrays):
    return tuple(pltpu.with_memory_space_constraint(x, pltpu.VMEM) for x in arrays)


def far(*arrays):
    return tuple(pltpu.with_memory_space_constraint(x, pltpu.HBM) for x in arrays)


def body(wave, potential):
    t = tables()
    rad = lax.axis_index("rad")
    ang = lax.axis_index("ang")
    core = ang % 2
    chip = ang // 2
    lane = jnp.arange(8, dtype=jnp.int32)
    edge = jnp.where(rad == 0, 15, 0)
    edge_uv = ((edge // 8) ^ core) * 8 + edge % 8
    idx = jnp.zeros(8, jnp.int32)
    for i, v in enumerate((rad, core, chip, rad * 2 + core, rad * 64 + core * 32 + chip, edge, edge_uv)):
        idx = jnp.where(lane == i, v.astype(jnp.int32), idx)

    sds = pltpu.VMEM
    wave, potential = far(wave, potential)
    rim = call(
        rim_kernel,
        idx,
        (wave, potential),
        [
            pl.BlockSpec((2, 2, 4, 8, NZ), lambda a, i: (0, 0, 0, i[5], 0)),
            pl.BlockSpec((4, 8, NZ), lambda a, i: (0, i[5], 0)),
        ],
        sds((16, 8 * NZ), f32),
        VM,
    )
    halo = lax.ppermute(rim, "rad", [(0, 1), (1, 0)])
    field = pltpu.HBM((2, 4, 2, LR, NZ), f32)
    lines = sds((1024, 128), f32)
    names = ("halo", "chip", "cell", "ah", "al", "fwd", "inv", "mid")
    stored = far(*(t[k] for k in names))
    shapes = [x.shape[1:] if k in ("chip", "cell", "mid") else x.shape for k, x in zip(names, stored)]
    targets = tuple(sds(shape, x.dtype) for shape, x in zip(shapes, stored))
    f, cs, uv, halo_table, chip_table, cell, ah, al, fwd, inv, mid = call(
        advance_kernel,
        idx,
        (wave, potential, *far(t["main"]), *stored),
        [ANY] * (3 + len(stored)),
        (
            pltpu.HBM((2, 2, 4, 2, 64, NZ), f32),
            pltpu.HBM((2, 2, 4, 64, NZ), f32),
            sds((2048, 128), f32),
        )
        + targets,
        (ANY, ANY, VM) + (VM,) * len(stored),
        scratch=(
            pltpu.VMEM((2, 2, 4, LR, NZ), f32),
            pltpu.VMEM((4, LR, NZ), f32),
            pltpu.VMEM((256, 768), bf16),
            pltpu.VMEM((2, 4, 2, LR, NZ), f32),
            pltpu.VMEM((2, 4, LR, NZ), f32),
            pltpu.VMEM((2, 2, 2, 256, NZ), bf16),
            pltpu.SemaphoreType.DMA((len(stored),)),
            pltpu.SemaphoreType.DMA((9,)),
            pltpu.SemaphoreType.DMA((24,)),
        ),
        flops=1 << 30,
        nbytes=5 << 20,
    )
    uv = call(
        halo_kernel,
        idx,
        near(halo, halo_table, cell, uv),
        [VM] * 4,
        sds((2048, 128), f32),
        VM,
        aliases={4: 0},
        flops=1 << 20,
        nbytes=1 << 20,
    )
    other = [(i, i ^ 1) for i in range(2 * CHIPS)]
    groups = [[2 * q + c for q in range(CHIPS)] for c in range(2)]
    exchange = functools.partial(
        lax.all_to_all, axis_name="ang", split_axis=0, concat_axis=0, tiled=True, axis_index_groups=groups
    )
    received = lax.ppermute(uv[1024:], "ang", other)
    UV, m = call(
        pair_kernel,
        idx,
        near(uv[:1024], received, chip_table),
        [VM] * 3,
        (lines, sds((512, 128), f32)),
        (VM, VM),
        flops=1 << 20,
        nbytes=2 << 20,
    )
    x = exchange(UV)
    y = call(
        middle_kernel,
        idx,
        near(x, fwd, inv, mid, ah, al),
        [VM] * 6,
        pltpu.HBM((CHIPS, 4, 8, 128), f32),
        ANY,
        scratch=(pltpu.VMEM((CHIPS, 4, 8, 128), f32), pltpu.SemaphoreType.DMA((2,))),
        flops=1 << 29,
        nbytes=3 << 20,
    ).reshape(lines.shape)
    w, mA, chip_table = call(
        local_kernel,
        idx,
        (*far(f, halo), *near(m), *[stored[i] for i in (2, 1, 3, 4, 0)], *far(y)),
        [ANY, ANY, VM] + [ANY] * 6,
        (sds(field.shape, f32), lines, sds((2, 64, 1, 128), f32)),
        (VM,) * 3,
        scratch=(
            pltpu.VMEM((LR, 128), f32),
            pltpu.VMEM((2, 64, 1, 128), f32),
            pltpu.VMEM(stored[3].shape, bf16),
            pltpu.VMEM(stored[4].shape, bf16),
            pltpu.VMEM((16, 8 * NZ), f32),
            pltpu.VMEM((2, 16, 16), f32),
            pltpu.VMEM((2, 2, 4, 2, 64, NZ), f32),
            pltpu.SemaphoreType.DMA((11,)),
        ),
        flops=3 << 30,
        nbytes=5 << 20,
    )
    y = exchange(y)
    near_cs = sds((2, 4, 64, NZ), f32)
    keep, send = call(
        spread_kernel,
        idx,
        near(y, mA, chip_table, w),
        [VM] * 4,
        (lines, lines),
        (VM,) * 2,
        flops=1 << 20,
        nbytes=5 << 20,
    )
    received = lax.ppermute(send, "ang", other)
    scratch = (pltpu.VMEM((2, 2, 4, 64, NZ), f32), pltpu.SemaphoreType.DMA((64 // CHUNK,)))
    whole_out = pltpu.HBM(wave.shape, f32)
    work = dict(flops=1 << 22, nbytes=6 << 20)
    out, cs_other, cell = call(
        finish_own_kernel,
        idx,
        (*near(w, keep), stored[2], *far(cs)),
        [VM] * 2 + [ANY] * 2,
        (whole_out, near_cs, targets[2]),
        (ANY, VM, VM),
        scratch=(*scratch[:1], pltpu.VMEM((2, 4, 64, NZ), f32), scratch[1], pltpu.SemaphoreType.DMA((3,))),
        **work,
    )
    return call(
        finish_other_kernel,
        idx,
        (*near(w, cs_other, received, cell), out),
        [VM] * 4 + [ANY],
        whole_out,
        ANY,
        scratch=scratch,
        aliases={5: 0},
        **work,
    )


def solution(mesh):
    placed = (P(None, None, "ang", "rad", None), P("ang", "rad", None))
    return jax.shard_map(
        body,
        mesh=mesh,
        in_specs=placed,
        out_specs=P(None, None, "ang", "rad", None),
        check_vma=False,
    )
```

```python
import functools

import jax
import jax.numpy as jnp
import numpy as np
from jax import lax
from jax.experimental import pallas as pl
from jax.experimental.pallas import tpu as pltpu
from jax.sharding import PartitionSpec as P

NA = 256
NR = 256
NZ = 256
CHIPS = 32
LR = 128
f32 = jnp.float32
bf16 = jnp.bfloat16
UNROLL = 2


def split(a):
    hi = np.asarray(a, np.float32).astype(jnp.bfloat16)
    lo = (np.asarray(a, np.float64) - hi.astype(np.float64)).astype(np.float32)
    return hi, lo.astype(jnp.bfloat16)


def coefficients():
    j = np.arange(NR, dtype=np.float32)
    radius = np.float32(1.0) + np.float32(9.0) * (j + np.float32(0.5)) / np.float32(NR)
    return (np.float32(100000.0) / (radius * radius)).astype(np.float64)


def radial_tables():
    lap = np.zeros((NR, NR))
    for d, c in ((0, -30.0), (1, 16.0), (2, -1.0)):
        for j in range(NR - d):
            lap[j, j + d] = c / 12.0
            lap[j + d, j] = c / 12.0
    k = 0.25 * lap
    even = np.eye(NR) - k @ k / 2.0
    odd = -k + k @ k @ k / 6.0
    main, halo = [], []
    for side in range(2):
        own = slice(LR * side, LR * side + LR)
        a, b = even[own, own], odd[own, own]
        hi, lo = split(np.block([[a, -b], [b, a]]))
        main.append(np.concatenate([hi, hi, lo], axis=1))
        rows = slice(120, 128) if side == 0 else slice(128, 136)
        cols = slice(128, 136) if side == 0 else slice(120, 128)
        a, b = even[rows, cols], odd[rows, cols]
        halo.append(np.block([[a, -b], [b, a]]))
    return np.stack(main), np.stack(halo).astype(np.float32)


def axial_tables():
    n = np.arange(1, NZ + 1)
    sine = np.sqrt(2.0 / (NZ + 1)) * np.sin(np.pi * (n[:, None] * n[None, :]) / (NZ + 1))
    s = 1.5 * (2.0 - 2.0 * np.cos(np.pi * n / (NZ + 1)))
    gain = (1.0 - 1j * s) / (1.0 + 1j * s)
    full = (sine * gain[None, :]) @ sine
    re, im = full.real, full.imag
    return split(np.stack([re, im - re, re + im]))


def dirichlet(c, size):
    off = 0.1 - 1j * c
    mat = np.zeros((size, size), complex)
    for t in range(size):
        mat[t, t] = 1.0 + 2j * c
        if t:
            mat[t, t - 1] = off
            mat[t - 1, t] = off
    inv = np.linalg.inv(mat)
    return inv, -off * inv[:, 0]


def angle_tables():
    cell = np.zeros((2, LR, 128), np.float32)
    chip = np.zeros((2, 2, 4, 64, 1, 128), np.float32)
    mid = np.zeros((2, 2, 32, 1, 128), np.float32)
    angle = np.arange(NA)
    second = 2.0 * np.cos(2.0 * np.pi * angle / NA) - 2.0
    for g, c in enumerate(coefficients()):
        rho = 0.1 / (0.1 - 1j * c)
        scale = 2.4 * (1.0 - rho)
        inv, p = dirichlet(c, 3)
        w0 = 2.0 * rho - 1.0
        values = [
            (p[0] + p[2]) / 2,
            (p[0] - p[2]) / 2,
            p[1],
            w0,
            (w0 + scale * (inv[0, 0] + inv[0, 2])) / 2,
            (w0 + scale * (inv[0, 0] - inv[0, 2])) / 2,
            scale * inv[0, 1],
            w0 + scale * inv[1, 1],
        ]
        side, j = divmod(g, LR)
        for k, value in enumerate(values):
            cell[side, j, 2 * k] = value.real
            cell[side, j, 2 * k + 1] = value.imag
        inv8, p8 = dirichlet(c, 7)
        core, jj = divmod(j, 64)
        middle, local = p8[3], scale * inv8[3, 3]
        for k, value in enumerate((middle.real, middle.imag, local.real, local.imag)):
            chip[side, core, k, jj] = value
        symbol = 1.0 / (1.2 + (0.1 - 1j * c) * second)
        coarse = scale * symbol.reshape(8, CHIPS).sum(0) / 8.0
        pos, r = divmod(jj, 2)
        mid[side, core, pos, 0, 64 * r : 64 * r + 32] = coarse.real
        mid[side, core, pos, 0, 64 * r + 32 : 64 * r + 64] = coarse.imag
    return cell, chip.reshape(4, 4, 64, 1, 128), mid.reshape(128, 1, 128)


def fourier_tables():
    k = np.arange(CHIPS)
    q = np.arange(CHIPS)
    fwd = np.zeros((2, 2, CHIPS, CHIPS, 2, 2, 2))
    inv = np.zeros((CHIPS, 2, 2, 2, 2, 2, CHIPS))
    for n in range(2):
        phase = -2.0 * np.pi * ((k[:, None] * (q[None, :] + n)) % CHIPS) / CHIPS
        e = np.exp(1j * phase)
        for s in range(2):
            fwd[0, s, :, :, n, 0, s] = e.real
            fwd[0, s, :, :, n, 1, s] = -e.imag
            fwd[1, s, :, :, n, 0, s] = e.imag
            fwd[1, s, :, :, n, 1, s] = e.real
            d = np.conj(e).T / CHIPS
            inv[:, n, 0, s, 0, s, :] = d.real
            inv[:, n, 0, s, 1, s, :] = -d.imag
            inv[:, n, 1, s, 0, s, :] = d.imag
            inv[:, n, 1, s, 1, s, :] = d.real
    fwd = fwd.reshape(128, 256)
    inv = inv.reshape(256, 128)
    fh, fl = split(fwd)
    ih, il = split(inv)
    return np.stack([fh, fl]), np.stack([ih, il])


@functools.cache
def tables():
    main, halo = radial_tables()
    ah, al = axial_tables()
    cell, chip, mid = angle_tables()
    fwd, inv = fourier_tables()
    return dict(main=main, halo=halo, ah=ah, al=al, cell=cell, chip=chip, mid=mid, fwd=fwd, inv=inv)


def dot(a, b):
    return jnp.dot(a, b, preferred_element_type=f32)


def halves(x):
    hi = x.astype(bf16)
    return hi, (x - hi.astype(f32)).astype(bf16)


def stacked(x):
    hi, lo = halves(x)
    return jnp.concatenate([hi, lo, hi], axis=0)


def times(x, high, low):
    hi, lo = halves(x)
    rows = x.shape[0]
    both = dot(jnp.concatenate([hi, lo], axis=0), high[...])
    return both[:rows] + both[rows:] + dot(hi, low[...])


def apply(table, x):
    hi, lo = halves(x)
    rows = table.shape[1]
    both = dot(table[...].reshape(2 * rows, table.shape[2]), hi)
    return both[:rows] + both[rows:] + dot(table[0], lo)


def complex_times(re, im, high, low):
    p, q, r = [times(x, high.at[i], low.at[i]) for i, x in enumerate((re + im, re, im))]
    return p - r, p + q


SIN = (-0.16666657119790096, 0.008333017866982043, -0.00019806657092710876, 2.600148052222563e-06)
COS = (
    -0.4999999955093015,
    0.041666640791225444,
    -0.0013888404392796263,
    2.476193429595472e-05,
    -2.607799377413178e-07,
)


def cos_sin(x):
    y = 0.5 * x
    q = y * y
    a = jnp.full_like(q, SIN[-1])
    for c in SIN[-2::-1]:
        a = a * q + c
    b = jnp.full_like(q, COS[-1])
    for c in COS[-2::-1]:
        b = b * q + c
    s = y + y * (q * a)
    c = 1.0 + q * b
    s2 = s + s
    return 1.0 - s2 * s, s2 * c


def cmul(cr, ci, x):
    return (cr * x[0] - ci * x[1], cr * x[1] + ci * x[0])


def add(x, y):
    return (x[0] + y[0], x[1] + y[1])


def sub(x, y):
    return (x[0] - y[0], x[1] - y[1])


def weights(coef, k, width):
    shape = (coef.shape[0], width)
    return tuple(jnp.broadcast_to(coef[:, i : i + 1], shape) for i in (2 * k, 2 * k + 1))


def reduce_cells(f, coef):
    width = f[0][0].shape[-1]
    s, d = add(f[1], f[3]), sub(f[1], f[3])
    even = add(cmul(*weights(coef, 0, width), s), cmul(*weights(coef, 2, width), f[2]))
    odd = cmul(*weights(coef, 1, width), d)
    return add(add(f[0], even), odd), sub(even, odd)


def advance_kernel(idx, w, pot, main, *refs):
    sources, (f_out, cs_out, uv), targets = refs[:8], refs[8:11], refs[11:19]
    w_in, pot_in, main_in, f, cs, staged, sems, in_sems, out_sems = refs[19:]
    own = {1: idx[3], 2: idx[0], 7: idx[4]}
    copies = [
        pltpu.make_async_copy(x.at[own[i]] if i in own else x, y, sems.at[i])
        for i, (x, y) in enumerate(zip(sources, targets))
    ]
    fetch_main = pltpu.make_async_copy(main.at[idx[0]], main_in, in_sems.at[8])
    fetches = [
        (
            pltpu.make_async_copy(pot.at[t], pot_in.at[t], in_sems.at[t]),
            pltpu.make_async_copy(w.at[:, :, t], w_in.at[:, :, t], in_sems.at[4 + t]),
        )
        for t in range(4)
    ]
    leaving = []
    for copy in fetches[0]:
        copy.start()
    fetch_main.start()
    for pair in fetches[1:]:
        for copy in pair:
            copy.start()
    for copy in copies:
        copy.start()

    def rotate(t):
        for row in range(0, LR, 16):
            rows, imag = slice(row, row + 16), slice(LR + row, LR + row + 16)
            c, s = cos_sin(pot_in[t, rows, :])
            cs[0, t, rows, :] = c
            cs[1, t, rows, :] = s
            for m in range(2):
                re, im = w_in[0, m, t, rows, :], w_in[1, m, t, rows, :]
                for at, x in ((rows, c * re + s * im), (imag, c * im - s * re)):
                    staged[t % 2, m, 0, at, :], staged[t % 2, m, 1, at, :] = halves(x)

    def multiply(t):
        for m in range(2):
            hi, lo = staged[t % 2, m, 0], staged[t % 2, m, 1]
            x = jnp.concatenate([hi, lo, hi], axis=0)
            f[m, t] = dot(main_in[...], x).reshape(2, LR, NZ)

    for t in range(5):
        if t < 4:
            for copy in fetches[t]:
                copy.wait()
        if t == 1:
            fetch_main.wait()
        if t > 0:
            multiply(t - 1)
        if t < 4:
            rotate(t)
        if t == 0:
            continue
        for j in range(2):
            rows = pl.ds(64 * j, 64)
            for m in range(2):
                leaving.append((f.at[m, t - 1, :, rows, :], f_out.at[m, j, t - 1]))
            leaving.append((cs.at[:, t - 1, rows, :], cs_out.at[j, :, t - 1]))
        first = len(leaving) - 6
        for i in range(6):
            leaving[first + i] = pltpu.make_async_copy(*leaving[first + i], out_sems.at[first + i])
            leaving[first + i].start()
    for copy in copies:
        copy.wait()
    coef = targets[2]

    def block(b, carry):
        rows = pl.ds(pl.multiple_of(b * 8, 8), 8)
        base = (lax.shift_right_logical(b, 3) ^ idx[1]) * 1024 + (b & 7) * 128
        k = coef[rows, :]
        for m in range(2):
            u, v = reduce_cells([(f[m, t, 0, rows, :], f[m, t, 1, rows, :]) for t in range(4)], k)
            for i, value in enumerate((u[0], u[1], v[0], v[1])):
                for z in range(2):
                    uv[pl.ds(base + 8 * z + 2 * i + m, 8, stride=16), :] = value[:, 128 * z : 128 * z + 128]
        return carry

    lax.fori_loop(0, 16, block, 0, unroll=UNROLL)
    for copy in leaving:
        copy.wait()


def rim_kernel(idx, w, pot, out):
    for t in range(4):
        c, s = cos_sin(pot[t])
        for m in range(2):
            re, im = w[0, m, t], w[1, m, t]
            x = jnp.concatenate([c * re + s * im, c * im - s * re], axis=0)
            out[:, (2 * t + m) * NZ : (2 * t + m + 1) * NZ] = x


def halo_part(table, halo):
    return jnp.dot(table, halo, precision=lax.Precision.HIGHEST, preferred_element_type=f32)


def halo_kernel(idx, halo, table, coef, uv_in, uv):
    edge_uv = idx[6] * 128
    out = halo_part(table[idx[0]], halo[...])
    k = coef[pl.ds(pl.multiple_of(idx[5] * 8, 8), 8), :]
    for m in range(2):
        cells = []
        for t in range(4):
            piece = out[:, (2 * t + m) * NZ : (2 * t + m + 1) * NZ]
            cells.append((piece[:8], piece[8:]))
        u, v = reduce_cells(cells, k)
        for i, value in enumerate((u[0], u[1], v[0], v[1])):
            for z in range(2):
                line = pl.ds(edge_uv + 8 * z + 2 * i + m, 8, stride=16)
                uv[line, :] = uv_in[line, :] + value[:, 128 * z : 128 * z + 128]


def row_swap(x, shift):
    return pltpu.roll(x, shift, 2)


def first_rows(core, shape):
    row = lax.broadcasted_iota(jnp.int32, shape, 2)
    return (lax.shift_right_logical(row, 2) ^ core) == 0


def tiles(x):
    return x.reshape(x.shape[0] // 16, 2, 8, 128)


def wide(x):
    x = tiles(x)
    rows = 8 * x.shape[0]
    return jnp.concatenate([x[:, z].reshape(rows, 128) for z in range(2)], axis=1)


def narrow(x):
    rows = x.shape[0] // 8
    return jnp.stack([x[:, 128 * z : 128 * z + 128].reshape(rows, 8, 128) for z in range(2)], axis=1)


def row_times(chip, k, x):
    shape = (64, 1, 8, 128)
    re = jnp.broadcast_to(chip[k].reshape(64, 1, 1, 128), shape)
    im = jnp.broadcast_to(chip[k + 1].reshape(64, 1, 1, 128), shape) * part_sign()
    return re * x + im * row_swap(x, 2)


def part_sign():
    row = lax.broadcasted_iota(jnp.int32, (1, 1, 8, 128), 2)
    return jnp.where((row & 2) == 0, -1.0, 1.0)


def pair_kernel(idx, own, received, chip, uv, m_out):
    a, b = tiles(own[...]), tiles(received[...])
    mask = first_rows(idx[1], a.shape)
    ends = jnp.where(mask, a, b)
    inner = jnp.where(mask, b, a)
    inner = inner + row_swap(inner, 4)
    low = first_rows(0, (1, 1, 8, 128))
    m_out[...] = jnp.where(low, inner[:32], inner[32:]).reshape(512, 128)
    uv[...] = (ends + row_times(chip, 0, inner)).reshape(uv.shape)


def local_kernel(idx, f, halo_far, m_rows, *refs):
    sources, after, out, mA = refs[:5], refs[5], refs[6], refs[7]
    chip, cell, chip_local, ah, al, halo, halo_table, g, sems = refs[8:]
    tables = [
        pltpu.make_async_copy(sources[0].at[idx[0]], cell, sems.at[4]),
        pltpu.make_async_copy(sources[1].at[idx[3], pl.ds(0, 2)], chip, sems.at[5]),
        pltpu.make_async_copy(sources[1].at[idx[3], pl.ds(2, 2)], chip_local, sems.at[10]),
        pltpu.make_async_copy(sources[2], ah, sems.at[6]),
        pltpu.make_async_copy(sources[3], al, sems.at[7]),
        pltpu.make_async_copy(sources[4], halo_table, sems.at[8]),
        pltpu.make_async_copy(halo_far, halo, sems.at[9]),
    ]
    copies = [pltpu.make_async_copy(f.at[m, j], g.at[m, j], sems.at[2 * m + j]) for m in range(2) for j in range(2)]
    for copy in tables + copies:
        copy.start()
    for copy in tables:
        copy.wait()

    halo[...] = halo_part(halo_table[idx[0]], halo[...])

    x = wide(m_rows[...])
    a = times(x, ah.at[0], al.at[0])
    b = a + times(x, ah.at[1], al.at[1])
    b = narrow(b)
    b = jnp.where(part_sign() < 0, -row_swap(b, 6), row_swap(b, 2))
    x = narrow(a) + b
    other, low = row_swap(x, 4), first_rows(0, (1, 1, 8, 128))
    x = jnp.concatenate([jnp.where(low, x, other), jnp.where(low, other, x)], axis=0)
    mA[...] = row_times(chip_local, 0, x).reshape(mA.shape)

    for m in range(2):
        for j in range(2):
            copies[2 * m + j].wait()

            @pl.when(idx[0] == 1 - j)
            def _():
                row = 56 * j
                for t in range(4):
                    at = slice((2 * t + m) * NZ, (2 * t + m + 1) * NZ)
                    for c in range(2):
                        g[m, j, t, c, row : row + 8, :] += halo[8 * c : 8 * c + 8, at]

            k = cell[64 * j : 64 * j + 64, :]
            cells = [(g[m, j, t, 0], g[m, j, t, 1]) for t in range(4)]
            s, d = add(cells[1], cells[3]), sub(cells[1], cells[3])
            even = add(cmul(*weights(k, 4, NZ), s), cmul(*weights(k, 6, NZ), cells[2]))
            odd = cmul(*weights(k, 5, NZ), d)
            parts = [
                cmul(*weights(k, 3, NZ), cells[0]),
                add(even, odd),
                add(cmul(*weights(k, 6, NZ), s), cmul(*weights(k, 7, NZ), cells[2])),
                sub(even, odd),
            ]
            re = jnp.concatenate([p[0] for p in parts], axis=0)
            im = jnp.concatenate([p[1] for p in parts], axis=0)
            re, im = complex_times(re, im, ah, al)
            for t in range(4):
                out[m, t, 0, 64 * j : 64 * j + 64, :] = re[t * 64 : (t + 1) * 64]
                out[m, t, 1, 64 * j : 64 * j + 64, :] = im[t * 64 : (t + 1) * 64]


def middle_kernel(idx, x, fwd, inv, mid, ah, al, out, y, sems):
    x = x[...].reshape(CHIPS, 4, 8, 128)
    x = jnp.concatenate([x[:, i].reshape(256, 128) for i in range(4)], axis=1)
    g = apply(fwd, x)
    k = jnp.broadcast_to(mid[...], (8, 128)).T
    rows = []
    for r in range(2):
        col = slice(r * NZ, (r + 1) * NZ)
        kr, ki = [
            jnp.concatenate([jnp.broadcast_to(k[64 * r + 32 * c : 64 * r + 32 * c + 32, 0:1], (32, NZ))] * 2, axis=0)
            for c in range(2)
        ]
        rows.append(cmul(kr, ki, (g[:64, col], g[64:, col])))
    re, im = complex_times(*[jnp.concatenate([p[c] for p in rows], axis=0) for c in range(2)], ah, al)
    copies = []
    for r in range(2):
        h = jnp.concatenate([x[64 * r : 64 * r + 64] for x in (re, im)], axis=0)
        part = apply(inv, h)
        for z in range(2):
            y[:, 2 * r + z] = part[:, 128 * z : 128 * z + 128].reshape(CHIPS, 8, 128)
        lines = pl.ds(2 * r, 2)
        copies.append(pltpu.make_async_copy(y.at[:, lines], out.at[:, lines], sems.at[r]))
        copies[-1].start()
    for copy in copies:
        copy.wait()


def fetch(row, cs, cs_out, sem):
    return pltpu.make_async_copy(cs.at[row], cs_out, sem)


def spread_kernel(idx, y, mA, chip, after, cell_far, keep, send, cell, sem):
    copy = pltpu.make_async_copy(cell_far.at[idx[0]], cell, sem)
    copy.start()
    x = tiles(y[...])
    total = x + row_swap(x, 4)
    inner = row_times(chip, 0, total) + tiles(mA[...])
    mask = first_rows(idx[1], x.shape)
    keep[...] = jnp.where(mask, x, inner).reshape(keep.shape)
    send[...] = jnp.where(mask, inner, x).reshape(keep.shape)
    copy.wait()


CHUNK = 16


CHUNK = 16


def gather_half(half, idx, w, y, coef, n):
    there = pl.ds(pl.multiple_of((idx[1] ^ half) * 64 + n * CHUNK, CHUNK), CHUNK)
    k = coef[there, :]
    for m in range(2):
        a = [
            jnp.concatenate(
                [y[pl.ds(n * CHUNK * 16 + 8 * z + 2 * i + m, CHUNK, stride=16), :] for z in range(2)], axis=1
            )
            for i in range(4)
        ]
        left, right = (a[0], a[1]), (a[2], a[3])
        s, d = add(left, right), sub(left, right)
        even = cmul(*weights(k, 0, NZ), s)
        odd = cmul(*weights(k, 1, NZ), d)
        parts = [left, add(even, odd), cmul(*weights(k, 2, NZ), s), sub(even, odd)]
        for t in range(4):
            yield m, t, w[m, t, 0, there, :] + parts[t][0], w[m, t, 1, there, :] + parts[t][1]


def rotate_out(o, cs, m, t, rows, re, im):
    c, s = cs[0, t, rows, :], cs[1, t, rows, :]
    o[0, m, t, rows, :] = c * re + s * im
    o[1, m, t, rows, :] = c * im - s * re


def leave(half, idx, o, out, sems, n):
    rows = pl.ds(n * CHUNK, CHUNK)
    there = pl.ds(pl.multiple_of((idx[1] ^ half) * 64 + n * CHUNK, CHUNK), CHUNK)
    return pltpu.make_async_copy(o.at[:, :, :, rows, :], out.at[:, :, :, there, :], sems.at[n])


def finish_own_kernel(idx, w, y, cell, cs_far, out, cs_other, o, cs_own, sems, more):
    copies = [fetch(idx[1] ^ i, cs_far, x, more.at[i]) for i, x in enumerate((cs_own, cs_other))]
    for copy in copies:
        copy.start()
    for n in range(64 // CHUNK):
        rows = slice(n * CHUNK, (n + 1) * CHUNK)
        for m, t, re, im in gather_half(0, idx, w, y, cell, n):
            o[0, m, t, rows, :] = re
            o[1, m, t, rows, :] = im
    copies[0].wait()
    for n in range(64 // CHUNK):
        rows = slice(n * CHUNK, (n + 1) * CHUNK)
        for m in range(2):
            for t in range(4):
                rotate_out(o, cs_own, m, t, rows, o[0, m, t, rows, :], o[1, m, t, rows, :])
        leave(0, idx, o, out, sems, n).start()
    for n in range(64 // CHUNK):
        leave(0, idx, o, out, sems, n).wait()
    copies[1].wait()


def finish_other_kernel(idx, w, cs, y, coef, before, out, o, sems):
    for n in range(64 // CHUNK):
        rows = slice(n * CHUNK, (n + 1) * CHUNK)
        for m, t, re, im in gather_half(1, idx, w, y, coef, n):
            rotate_out(o, cs, m, t, rows, re, im)
        leave(1, idx, o, out, sems, n).start()
    for n in range(64 // CHUNK):
        leave(1, idx, o, out, sems, n).wait()


def call(kernel, idx, args, in_specs, out_shape, out_specs, grid=(1,), scratch=(), aliases=None, flops=0, nbytes=0):
    return pl.pallas_call(
        kernel,
        out_shape=out_shape,
        grid_spec=pltpu.PrefetchScalarGridSpec(
            num_scalar_prefetch=1, grid=grid, in_specs=in_specs, out_specs=out_specs, scratch_shapes=scratch
        ),
        input_output_aliases=aliases or {},
        compiler_params=pltpu.CompilerParams(
            dimension_semantics=("arbitrary",) * len(grid), vmem_limit_bytes=24 << 20
        ),
        cost_estimate=pl.CostEstimate(flops=flops, bytes_accessed=nbytes, transcendentals=0),
        name=kernel.__name__,
    )(idx, *args)


def whole(shape):
    return pl.BlockSpec(shape, lambda *_: (0,) * len(shape))


VM = pl.BlockSpec(memory_space=pltpu.VMEM)
ANY = pl.BlockSpec(memory_space=pl.ANY)


def near(*arrays):
    return tuple(pltpu.with_memory_space_constraint(x, pltpu.VMEM) for x in arrays)


def far(*arrays):
    return tuple(pltpu.with_memory_space_constraint(x, pltpu.HBM) for x in arrays)


def body(wave, potential):
    t = tables()
    rad = lax.axis_index("rad")
    ang = lax.axis_index("ang")
    core = ang % 2
    chip = ang // 2
    lane = jnp.arange(8, dtype=jnp.int32)
    edge = jnp.where(rad == 0, 15, 0)
    edge_uv = ((edge // 8) ^ core) * 8 + edge % 8
    idx = jnp.zeros(8, jnp.int32)
    for i, v in enumerate((rad, core, chip, rad * 2 + core, rad * 64 + core * 32 + chip, edge, edge_uv)):
        idx = jnp.where(lane == i, v.astype(jnp.int32), idx)

    sds = pltpu.VMEM
    wave, potential = far(wave, potential)
    rim = call(
        rim_kernel,
        idx,
        (wave, potential),
        [
            pl.BlockSpec((2, 2, 4, 8, NZ), lambda a, i: (0, 0, 0, i[5], 0)),
            pl.BlockSpec((4, 8, NZ), lambda a, i: (0, i[5], 0)),
        ],
        sds((16, 8 * NZ), f32),
        VM,
    )
    halo = lax.ppermute(rim, "rad", [(0, 1), (1, 0)])
    field = pltpu.HBM((2, 4, 2, LR, NZ), f32)
    lines = sds((1024, 128), f32)
    names = ("halo", "chip", "cell", "ah", "al", "fwd", "inv", "mid")
    stored = far(*(t[k] for k in names))
    shapes = [x.shape[1:] if k in ("chip", "cell", "mid") else x.shape for k, x in zip(names, stored)]
    targets = tuple(sds(shape, x.dtype) for shape, x in zip(shapes, stored))
    f, cs, uv, halo_table, chip_table, cell, ah, al, fwd, inv, mid = call(
        advance_kernel,
        idx,
        (wave, potential, *far(t["main"]), *stored),
        [ANY] * (3 + len(stored)),
        (
            pltpu.HBM((2, 2, 4, 2, 64, NZ), f32),
            pltpu.HBM((2, 2, 4, 64, NZ), f32),
            sds((2048, 128), f32),
        )
        + targets,
        (ANY, ANY, VM) + (VM,) * len(stored),
        scratch=(
            pltpu.VMEM((2, 2, 4, LR, NZ), f32),
            pltpu.VMEM((4, LR, NZ), f32),
            pltpu.VMEM((256, 768), bf16),
            pltpu.VMEM((2, 4, 2, LR, NZ), f32),
            pltpu.VMEM((2, 4, LR, NZ), f32),
            pltpu.VMEM((2, 2, 2, 256, NZ), bf16),
            pltpu.SemaphoreType.DMA((len(stored),)),
            pltpu.SemaphoreType.DMA((9,)),
            pltpu.SemaphoreType.DMA((24,)),
        ),
        flops=1 << 30,
        nbytes=5 << 20,
    )
    uv = call(
        halo_kernel,
        idx,
        near(halo, halo_table, cell, uv),
        [VM] * 4,
        sds((2048, 128), f32),
        VM,
        aliases={4: 0},
        flops=1 << 20,
        nbytes=1 << 20,
    )
    other = [(i, i ^ 1) for i in range(2 * CHIPS)]
    groups = [[2 * q + c for q in range(CHIPS)] for c in range(2)]
    exchange = functools.partial(
        lax.all_to_all, axis_name="ang", split_axis=0, concat_axis=0, tiled=True, axis_index_groups=groups
    )
    received = lax.ppermute(uv[1024:], "ang", other)
    UV, m = call(
        pair_kernel,
        idx,
        near(uv[:1024], received, chip_table),
        [VM] * 3,
        (lines, sds((512, 128), f32)),
        (VM, VM),
        flops=1 << 20,
        nbytes=2 << 20,
    )
    x = exchange(UV)
    y = call(
        middle_kernel,
        idx,
        near(x, fwd, inv, mid, ah, al),
        [VM] * 6,
        pltpu.HBM((CHIPS, 4, 8, 128), f32),
        ANY,
        scratch=(pltpu.VMEM((CHIPS, 4, 8, 128), f32), pltpu.SemaphoreType.DMA((2,))),
        flops=1 << 29,
        nbytes=3 << 20,
    ).reshape(lines.shape)
    w, mA, chip_table = call(
        local_kernel,
        idx,
        (*far(f, halo), *near(m), *[stored[i] for i in (2, 1, 3, 4, 0)], *far(y)),
        [ANY, ANY, VM] + [ANY] * 6,
        (sds(field.shape, f32), lines, sds((2, 64, 1, 128), f32)),
        (VM,) * 3,
        scratch=(
            pltpu.VMEM((LR, 128), f32),
            pltpu.VMEM((2, 64, 1, 128), f32),
            pltpu.VMEM(stored[3].shape, bf16),
            pltpu.VMEM(stored[4].shape, bf16),
            pltpu.VMEM((16, 8 * NZ), f32),
            pltpu.VMEM((2, 16, 16), f32),
            pltpu.VMEM((2, 2, 4, 2, 64, NZ), f32),
            pltpu.SemaphoreType.DMA((11,)),
        ),
        flops=3 << 30,
        nbytes=5 << 20,
    )
    y = exchange(y)
    near_cs = sds((2, 4, 64, NZ), f32)
    keep, send, cell = call(
        spread_kernel,
        idx,
        (*near(y, mA, chip_table, w), stored[2]),
        [VM] * 4 + [ANY],
        (lines, lines, targets[2]),
        (VM,) * 3,
        scratch=(pltpu.SemaphoreType.DMA,),
        flops=1 << 20,
        nbytes=5 << 20,
    )
    received = lax.ppermute(send, "ang", other)
    scratch = (pltpu.VMEM((2, 2, 4, 64, NZ), f32), pltpu.SemaphoreType.DMA((64 // CHUNK,)))
    whole_out = pltpu.HBM(wave.shape, f32)
    work = dict(flops=1 << 22, nbytes=6 << 20)
    out, cs_other = call(
        finish_own_kernel,
        idx,
        (*near(w, keep, cell), *far(cs)),
        [VM] * 3 + [ANY],
        (whole_out, near_cs),
        (ANY, VM),
        scratch=(*scratch[:1], pltpu.VMEM((2, 4, 64, NZ), f32), scratch[1], pltpu.SemaphoreType.DMA((2,))),
        **work,
    )
    return call(
        finish_other_kernel,
        idx,
        (*near(w, cs_other, received, cell), out),
        [VM] * 4 + [ANY],
        whole_out,
        ANY,
        scratch=scratch,
        aliases={5: 0},
        **work,
    )


def solution(mesh):
    placed = (P(None, None, "ang", "rad", None), P("ang", "rad", None))
    return jax.shard_map(
        body,
        mesh=mesh,
        in_specs=placed,
        out_specs=P(None, None, "ang", "rad", None),
        check_vma=False,
    )
```
